32 devices in a mesh: groups: 2 (over x), chan: 16 (over z, y, core).
Axes of the slice: x: 2, y: 2, z: 4, core: 2. Of those that a mesh axis runs over, the one named last changes fastest.
Arguments:
- spectra: bfloat16 [2, 8, 512, 512], P(None, 'groups', 'chan'), parts along dimension 1, may hold values from -6 to 6
- filter_bank: float32 [2, 8, 65], replicated, may hold values from -0.5 to 0.5
- band_index: int32 [512], replicated, may hold values from 0 to 7
- window_mask: int32 [8, 512], P('groups', 'chan'), parts along dimension 0, may hold values 0 or 1
- owner_order: int32 [8], P('groups'), parts along dimension 0, may hold values from 0 to 15, as said below
- source_offset: int32 [8, 32], P('groups'), parts along dimension 0, may hold values from 0 to 31, each once within a row
Outputs:
- cross: bfloat16 [2, 256, 512, 512], P(None, 'groups', 'chan'), parts along dimension 1
The draws below stay inside these ranges and needn't reach their ends.
There are 2 independent parts, one for each index of `groups`. The reference program is written for one: setup_inputs(seed, part) draws one part's arguments, and reference() takes and returns one part's arrays. A program takes and returns all parts, laid end to end along the dimension named above; an argument that names none is the same for every part. Nothing has to cross between parts.
Inputs may be any that keep to these rules, and one draw needn't show every extreme that they name: `owner_order`: 4 distinct device indices, below 16.
All inputs are finite; a program needn't handle non-finite values. No bound on the sum of `window_mask` on one device may be relied on, other than what follows from the above.
Results may differ from the reference program's by a relative error of at most 0.0057.
Values may be sent and summed in bfloat16 or wider, within the bound.
A program may use at most 192 MiB of HBM per device.

```python
import jax
import jax.numpy as jnp
from jax import lax

F = 512
CH_DEV = 32
WIN = 4
TAPS = 65
NBANK = 8
SMOOTH = 17
ROUNDS = 4
CHANNELS = 512
N_CHAN = 16


def draw_owner_order(key, part):
    devices = CHANNELS // CH_DEV
    first, second = jax.random.split(key)
    middle = 1 + jax.random.permutation(first, devices - 2)[:ROUNDS - 2]
    chosen = jnp.concatenate([jnp.array([0, devices - 1], jnp.int32), middle.astype(jnp.int32)])
    order = jax.random.permutation(second, ROUNDS)
    return chosen[order].astype(jnp.int32)


def plant(entries, key, least, largest):
    index_at = [jax.random.randint(jax.random.fold_in(key, axis), (), 0, length) for axis, length in enumerate(entries.shape)]
    longest = entries.shape.index(max(entries.shape))
    beside = index_at[:longest] + [(index_at[longest] + 1) % entries.shape[longest]] + index_at[longest + 1:]
    return entries.at[tuple(index_at)].set(least).at[tuple(beside)].set(largest)


def level_of(stream_key, dims, cuts, smallest, top_value):
    def one(dim, parts):
        steps = jax.random.uniform(jax.random.fold_in(jax.random.fold_in(stream_key, 6), dim), (parts,), jnp.float32, smallest / len(cuts), top_value / len(cuts))
        return jnp.repeat(jnp.exp(steps), dims[dim] // parts).reshape((-1,) + (1,) * (len(dims) - dim - 1))

    factor_of = one(*cuts[0])
    for cut in cuts[1:]:
        factor_of = factor_of * one(*cut)
    return factor_of


def gaussian(key, dims, deviation, limit, cuts=(), kind=jnp.bfloat16):
    entries = jax.random.normal(key, dims, jnp.float32) * deviation
    if len(cuts) > 0:
        entries = level_of(key, dims, cuts, -0.22, 0.18) * entries
    return jnp.clip(entries, min=-limit, max=limit).astype(kind)


def setup_inputs(seed: int = 0, part: int = 0) -> dict:
    key_of = jax.random.split(jax.random.key(seed), 7)
    part_splits = jax.random.split(jax.random.fold_in(key_of[6], part), 7)
    return {
        "spectra": gaussian(part_splits[0], (2, WIN, CHANNELS, F), 1.0, 6.0, ((2, 16),)),
        "filter_bank": gaussian(key_of[1], (2, NBANK, TAPS), (2 * TAPS) ** -0.5, 0.5, (), jnp.float32),
        "band_index": plant(jax.random.randint(key_of[2], (F,), 0, NBANK), jax.random.fold_in(key_of[2], 1), 0, NBANK - 1).astype(jnp.int32),
        "window_mask": plant((jax.random.randint(part_splits[3], (WIN, CHANNELS), 0, 8) < 7).astype(jnp.int32), jax.random.fold_in(part_splits[3], 1), 0, 1),
        "owner_order": draw_owner_order(jax.random.fold_in(jax.random.fold_in(key_of[6], part), 71), part),
        "source_offset": jax.vmap(lambda own: jax.random.permutation(own, CH_DEV))(jax.random.split(part_splits[5], ROUNDS)).reshape((ROUNDS, CH_DEV)).astype(jnp.int32),
    }


water_level = 0.05

def filter_taps(filter_bank, band_index):
    choose = (band_index[:, None] == jnp.arange(NBANK, dtype=jnp.int32)[None, :]).astype(jnp.float32)
    return jnp.einsum('fb,pbk->pkf', choose, filter_bank, precision=lax.Precision.HIGHEST)

def velocity_whiten(padded, taps, window_mask):
    count = padded.shape[2] - (TAPS - 1)
    real_sum = jnp.zeros((padded.shape[1], count, padded.shape[3]), jnp.float32)
    imag_sum = jnp.zeros((padded.shape[1], count, padded.shape[3]), jnp.float32)
    for tap_pos in range(TAPS):
        real_in = padded[0, :, tap_pos:tap_pos + count]
        imag_in = padded[1, :, tap_pos:tap_pos + count]
        real_sum = real_sum + taps[0, tap_pos] * real_in - taps[1, tap_pos] * imag_in
        imag_sum = imag_sum + taps[0, tap_pos] * imag_in + taps[1, tap_pos] * real_in
    power = real_sum * real_sum + imag_sum * imag_sum
    reach = SMOOTH // 2
    padded_power = jnp.pad(power, ((0, 0), (0, 0), (reach, reach)))
    smooth = jnp.zeros_like(power)
    for shift_pos in range(SMOOTH):
        smooth = smooth + padded_power[:, :, shift_pos:shift_pos + power.shape[2]]
    smooth = smooth / SMOOTH
    scale = lax.rsqrt(smooth + water_level) * window_mask.astype(jnp.float32)[:, :, None]
    return jnp.stack([real_sum * scale, imag_sum * scale]).astype(jnp.bfloat16)

def cross_block(source, whitened):
    src_real = source[0].astype(jnp.float32)
    src_imag = source[1].astype(jnp.float32)
    loc_real = whitened[0].astype(jnp.float32)
    loc_imag = whitened[1].astype(jnp.float32)
    real_out = jnp.einsum('wsf,wcf->scf', src_real, loc_real) + jnp.einsum('wsf,wcf->scf', src_imag, loc_imag)
    imag_out = jnp.einsum('wsf,wcf->scf', src_real, loc_imag) - jnp.einsum('wsf,wcf->scf', src_imag, loc_real)
    return (jnp.stack([real_out, imag_out]) / WIN).astype(jnp.bfloat16)

def reference(spectra, filter_bank, band_index, window_mask, owner_order, source_offset):
    half_width = TAPS // 2
    taps = filter_taps(filter_bank, band_index)
    padded = jnp.pad(spectra.astype(jnp.float32), ((0, 0), (0, 0), (half_width, half_width), (0, 0)))
    whitened = velocity_whiten(padded, taps, window_mask)
    channel_index = (owner_order[:, None] * CH_DEV + source_offset).reshape(-1).astype(jnp.int32)
    picked = whitened[:, :, channel_index, :]
    picked = picked.reshape(2, WIN, ROUNDS, CH_DEV, F).transpose(2, 0, 1, 3, 4)
    blocks = lax.map(lambda source: cross_block(source, whitened), picked)
    return blocks.transpose(1, 0, 2, 3, 4).reshape(2, ROUNDS * CH_DEV, CH_DEV * N_CHAN, F)
```

```python
import functools

import jax
import jax.numpy as jnp
from jax import lax
from jax.experimental import pallas as pl
from jax.experimental.pallas import tpu as pltpu
from jax.sharding import PartitionSpec as P

SMOOTH = 17
water_level = 0.05
bf16 = jnp.bfloat16
f32 = jnp.float32
LANES = 128
LAG = 4


def split(x):
    hi = x.astype(bf16)
    return hi, (x - hi.astype(f32)).astype(bf16)


def build_toeplitz(bank_ref, toep):
    _, nbank, ntap = bank_ref.shape
    chans = toep.shape[1] // (2 * nbank)
    for b in range(nbank):
        parts = []
        for p in range(2):
            row = jnp.concatenate(
                [bank_ref[p, b : b + 1, :], jnp.zeros((1, LANES - ntap), f32)], axis=1
            )
            full = jnp.broadcast_to(row, (chans, LANES))
            parts.append(split(pltpu.roll(full, 0, 1, stride=1, stride_axis=0)))
        at = b * 2 * chans
        for part in range(2):
            real, imag = parts[0][part], parts[1][part]
            toep[part, at : at + chans, :LANES] = real
            toep[part, at : at + chans, LANES:] = -imag
            toep[part, at + chans : at + 2 * chans, :LANES] = imag
            toep[part, at + chans : at + 2 * chans, LANES:] = real


def build_window(band):
    bins = band.shape[0]
    rows = lax.broadcasted_iota(jnp.int32, (bins, bins), 0)
    cols = lax.broadcasted_iota(jnp.int32, (bins, bins), 1)
    band[...] = (jnp.abs(rows - cols) <= SMOOTH // 2).astype(f32).astype(bf16)


def filter_window(nbank, w, x, toep, index_ref, filt, power):
    bins = filt.shape[2]
    chans = toep.shape[1] // (2 * nbank)
    tile = 256
    rows = slice(w * chans, (w + 1) * chans)
    for n in range(bins // tile):
        cut = slice(n * tile, (n + 1) * tile)
        here = x(cut)
        res = jnp.dot(toep[0], here, preferred_element_type=f32)
        res += jnp.dot(toep[1], here, preferred_element_type=f32)
        index = index_ref[:, cut]
        acc = res[: 2 * chans]
        for b in range(1, nbank):
            acc = jnp.where(index == b, res[2 * chans * b : 2 * chans * (b + 1)], acc)
        real, imag = acc[:chans], acc[chans:]
        filt[0, rows, cut] = real
        filt[1, rows, cut] = imag
        hi, lo = split(real * real + imag * imag)
        power[0, rows, cut] = hi
        power[1, rows, cut] = lo


def whiten_window(w, band, mask_ref, filt, power):
    chans = mask_ref.shape[1]
    rows = slice(w * chans, (w + 1) * chans)
    smooth = jnp.dot(power[0, rows], band[...], preferred_element_type=f32)
    smooth += jnp.dot(power[1, rows], band[...], preferred_element_type=f32)
    scale = lax.rsqrt(smooth * (1.0 / SMOOTH) + water_level)
    eye = lax.broadcasted_iota(jnp.int32, (chans, chans), 0) == lax.broadcasted_iota(
        jnp.int32, (chans, chans), 1
    )
    row = jnp.broadcast_to(mask_ref[w : w + 1, :].astype(f32), (chans, chans))
    valid = jnp.sum(jnp.where(eye, row, 0.0), axis=1, keepdims=True)
    scale = scale * valid
    return [(filt[p, rows] * scale).astype(bf16) for p in range(2)]


class Line:
    def __init__(self, pos, length, device_of, lag, refs):
        self.pos, self.length, self.device_of, self.lag = pos, length, device_of, lag
        self.own, self.out_r, self.out_l, self.in_r, self.in_l, self.sems = refs
        self.count = self.own.shape[0]

    def clear(self):
        @pl.when(self.pos == 0)
        def _():
            self.in_r[...] = jnp.zeros_like(self.in_r)

        @pl.when(self.pos == self.length - 1)
        def _():
            self.in_l[...] = jnp.zeros_like(self.in_l)

    def copy(self, way, k):
        out, into = (self.out_r, self.in_r) if way == 0 else (self.out_l, self.in_l)
        other = self.pos + 1 if way == 0 else self.pos - 1
        return pltpu.make_async_remote_copy(
            src_ref=out.at[k],
            dst_ref=into.at[k],
            send_sem=self.sems.at[way, 0, k],
            recv_sem=self.sems.at[way, 1, k],
            device_id={"chan": self.device_of(other)},
            device_id_type=pl.DeviceIdType.MESH,
        )

    def tick(self, t):
        for way in range(2):
            behind = self.pos if way == 0 else self.length - 1 - self.pos
            out, into = (self.out_r, self.in_r) if way == 0 else (self.out_l, self.in_l)
            k = t - self.lag * behind
            inside = jnp.logical_and(k >= 0, k < self.count)

            @pl.when(jnp.logical_and(inside, behind > 0))
            def _(way=way, k=k):
                self.copy(way, k).wait_recv()

            @pl.when(jnp.logical_and(inside, behind < self.length - 1))
            def _(way=way, k=k, out=out, into=into):
                out[k] = self.own[k] + into[k]
                self.copy(way, k).start()

    def result(self, k):
        return self.own[k] + self.in_r[k] + self.in_l[k]

    def drain(self):
        for way in range(2):
            behind = self.pos if way == 0 else self.length - 1 - self.pos

            @pl.when(behind < self.length - 1)
            def _(way=way):
                @pl.loop(0, self.count)
                def _(k):
                    self.copy(way, k).wait_send()


def front_kernel(
    rows,
    cols,
    owner_ref,
    own_ref,
    bank_ref,
    index_ref,
    mask_ref,
    out_ref,
    src_ref,
    halo,
    toep,
    band,
    filt,
    power,
    mine,
    beside,
    row_buf,
    done,
    gathered,
    halo_sems,
    beside_sems,
    row_sems,
    gather_sems,
):
    wins, chans = mask_ref.shape
    bins = own_ref.shape[3]
    parts = 2 * cols
    subs, piece = beside.shape[1], beside.shape[2]
    me = lax.axis_index("chan")
    size = rows * cols * 2
    core = me % 2
    place = me % (2 * cols)
    base = me - place
    row = me // (2 * cols)
    partner = me + 1 - 2 * core
    mesh_id = pl.DeviceIdType.MESH

    barrier = pltpu.get_barrier_semaphore()
    partners = [
        (me > 0, me - 1),
        (me < size - 1, me + 1),
        (row > 0, me - 2 * cols),
        (row < rows - 1, me + 2 * cols),
    ] + [(place != j, base + j) for j in range(2 * cols)]
    expected = jnp.int32(0)
    for there, who in partners:
        expected += there.astype(jnp.int32)

        @pl.when(there)
        def _(who=who):
            pl.semaphore_signal(barrier, inc=1, device_id={"chan": who}, device_id_type=mesh_id)

    pl.semaphore_wait(barrier, expected)

    def halo_copy(way, w):
        return pltpu.make_async_remote_copy(
            src_ref=own_ref.at[:, w],
            dst_ref=halo.at[way, :, w],
            send_sem=halo_sems.at[way, 0, w],
            recv_sem=halo_sems.at[way, 1, w],
            device_id={"chan": me + 1 - 2 * way},
            device_id_type=mesh_id,
        )

    order = list(range(wins))
    sends = (me < size - 1, me > 0)
    for w in order:
        for way in range(2):

            @pl.when(sends[way])
            def _(way=way, w=w):
                halo_copy(way, w).start()

    for way in range(2):

        @pl.when(jnp.logical_not(sends[1 - way]))
        def _(way=way):
            halo[way] = jnp.zeros_like(halo[way])

    line = Line(row, rows, lambda i: i * 2 * cols + place, LAG, (*row_buf, row_sems))
    line.clear()
    build_toeplitz(bank_ref, toep)
    build_window(band)

    def beside_copy(sender, j):
        return pltpu.make_async_remote_copy(
            src_ref=mine.at[pl.ds(j * subs, subs)],
            dst_ref=beside.at[sender],
            send_sem=beside_sems.at[0, j],
            recv_sem=beside_sems.at[1, sender],
            device_id={"chan": base + j},
            device_id_type=mesh_id,
        )

    blank = jnp.zeros((LANES - 3 * chans, bins), bf16)
    for w in order:
        for way in range(2):

            @pl.when(sends[1 - way])
            def _(way=way, w=w):
                halo_copy(way, w).wait_recv()

        def x(cut, w=w):
            stack = []
            for p in range(2):
                stack += [halo[0, p, w, :, cut], own_ref[p, w, :, cut], halo[1, p, w, :, cut]]
                stack += [blank[:, cut]]
            return jnp.concatenate(stack, axis=0)

        filter_window(bank_ref.shape[1], w, x, toep, index_ref, filt, power)
        white = whiten_window(w, band, mask_ref, filt, power)
        for p in range(2):
            out_ref[p, w] = white[p]
            for i in range(chans // piece):
                mine[(w * 2 + p) * (chans // piece) + i] = white[p][i * piece : (i + 1) * piece]
        for j in range(w * parts // wins, (w + 1) * parts // wins):

            @pl.when(place != j)
            def _(j=j):
                beside_copy(place, j).start()

    beside[place] = mine[pl.ds(place * subs, subs)]
    for j in range(parts):

        @pl.when(place != j)
        def _(j=j):
            beside_copy(j, j).wait_recv()

    count = line.count

    @pl.loop(0, count)
    def _(k):
        total = jnp.zeros((piece, bins), bf16)
        for j in range(parts):
            total += beside[j, k % subs] * (owner_ref[k // subs] == base + j).astype(f32).astype(bf16)
        line.own[k] = total

    def give(src, origin, k, sem, who):
        return pltpu.make_async_remote_copy(
            src_ref=src,
            dst_ref=gathered.at[origin, k],
            send_sem=gather_sems.at[sem, k],
            recv_sem=gather_sems.at[2 * parts + origin, k],
            device_id={"chan": who},
            device_id_type=mesh_id,
        )

    def put(j, k, value):
        src_ref[k // subs, j * subs + k % subs] = value

    alike = [jnp.logical_and(place != j, core == j % 2) for j in range(parts)]
    last = LAG * (rows - 1)

    @pl.loop(0, count + last + LAG)
    def _(t):
        line.tick(t)
        k = t - last

        @pl.when(jnp.logical_and(k >= 0, k < count))
        def _():
            total = line.result(k)
            done[k] = total
            for j in range(parts):

                @pl.when(alike[j])
                def _(j=j):
                    give(done.at[k], place, k, j, base + j).start()

            give(done.at[k], place, k, parts + place, partner).start()
            put(place, k, total)

        q = t - last - LAG

        @pl.when(q >= 0)
        def _():
            for j in range(parts):

                @pl.when(alike[j])
                def _(j=j):
                    give(done.at[q], j, q, j, partner).wait_recv()
                    give(gathered.at[j, q], j, q, parts + j, partner).start()
                    put(j, q, gathered[j, q])

    @pl.loop(0, count)
    def _(k):
        for j in range(parts):

            @pl.when(core != j % 2)
            def _(j=j):
                give(done.at[k], j, k, j, partner).wait_recv()
                put(j, k, gathered[j, k])

    for way in range(2):
        for w in range(wins):

            @pl.when(sends[way])
            def _(way=way, w=w):
                halo_copy(way, w).wait_send()

    for j in range(parts):

        @pl.when(place != j)
        def _(j=j):
            beside_copy(place, j).wait_send()

    line.drain()

    @pl.loop(0, count)
    def _(k):
        give(done.at[k], place, k, parts + place, partner).wait_send()
        for j in range(parts):

            @pl.when(alike[j])
            def _(j=j):
                give(done.at[k], place, k, j, partner).wait_send()
                give(gathered.at[j, k], j, k, parts + j, partner).wait_send()


def front(grid, owner, own, bank, index, mask):
    _, wins, chans, bins = own.shape
    nbank = bank.shape[1]
    rounds = owner.shape[0]
    rows, cols = grid
    parts = 2 * cols
    total = wins * 2 * chans
    piece = min(chans, total // parts)
    subs = total // parts // piece
    count = rounds * subs
    vmem = pl.BlockSpec(memory_space=pltpu.VMEM)
    chunk = (piece, bins)
    chunks = pltpu.VMEM((count, *chunk), bf16)
    return pl.pallas_call(
        functools.partial(front_kernel, rows, cols),
        out_shape=[
            jax.ShapeDtypeStruct(own.shape, bf16),
            jax.ShapeDtypeStruct((rounds, parts * subs, piece, bins), bf16),
        ],
        in_specs=[pl.BlockSpec(memory_space=pltpu.SMEM)] + [vmem] * 4,
        out_specs=[vmem] * 2,
        scratch_shapes=[
            pltpu.VMEM((2, *own.shape), bf16),
            pltpu.VMEM((2, nbank * 2 * chans, 2 * LANES), bf16),
            pltpu.VMEM((bins, bins), bf16),
            pltpu.VMEM((2, wins * chans, bins), f32),
            pltpu.VMEM((2, wins * chans, bins), bf16),
            pltpu.VMEM((parts * subs, *chunk), bf16),
            pltpu.VMEM((parts, subs, *chunk), bf16),
            [chunks] * 5,
            chunks,
            pltpu.VMEM((parts, count, *chunk), bf16),
            pltpu.SemaphoreType.DMA((2, 2, wins)),
            pltpu.SemaphoreType.DMA((2, parts)),
            pltpu.SemaphoreType.DMA((2, 2, count)),
            pltpu.SemaphoreType.DMA((3 * parts, count)),
        ],
        compiler_params=pltpu.CompilerParams(collective_id=0, has_side_effects=True),
        name="front",
    )(owner, own, bank, index, mask)


def tree_sum(terms):
    while len(terms) > 1:
        terms = [a + b for a, b in zip(terms[::2], terms[1::2])]
    return terms[0]


def cross_kernel(offset_ref, src_ref, loc_ref, out_ref, wide, held):
    _, wins, chans, bins = loc_ref.shape
    count = out_ref.shape[1]
    r, h = pl.program_id(0), pl.program_id(1)

    @pl.when(jnp.logical_and(r == 0, h == 0))
    def _():
        held[...] = loc_ref[...]

    @pl.when(h == 0)
    def _():
        for p in range(2):
            for w in range(wins):
                wide[:, p * wins + w, :] = src_ref[0, w, p].astype(f32) * (1.0 / wins)

    for n in range(bins // LANES):
        cut = slice(n * LANES, (n + 1) * LANES)

        def one(j, carry, cut=cut):
            loc = [[held[p, w, :, cut] for w in range(wins)] for p in range(2)]
            at = offset_ref[r, h * count + j]
            src = [
                [
                    jnp.broadcast_to(
                        wide[at, p * wins + w : p * wins + w + 1, cut], (chans, LANES)
                    ).astype(bf16)
                    for w in range(wins)
                ]
                for p in range(2)
            ]
            real = tree_sum(
                [src[p][w] * loc[p][w] for w in range(wins) for p in range(2)]
            )
            plus = tree_sum([src[0][w] * loc[1][w] for w in range(wins)])
            minus = tree_sum([src[1][w] * loc[0][w] for w in range(wins)])
            out_ref[0, j, :, cut] = real
            out_ref[1, j, :, cut] = plus - minus
            return carry

        lax.fori_loop(0, count, one, 0, unroll=4)


def cross(offset, src, loc, blocks=1):
    rounds, wins, _, chans, bins = src.shape
    per = chans // blocks
    return pl.pallas_call(
        cross_kernel,
        out_shape=jax.ShapeDtypeStruct((2, rounds * chans, chans, bins), bf16),
        grid=(rounds, blocks),
        in_specs=[
            pl.BlockSpec(memory_space=pltpu.SMEM),
            pl.BlockSpec((1, wins, 2, chans, bins), lambda r, h: (r, 0, 0, 0, 0)),
            pl.BlockSpec((2, wins, chans, bins), lambda r, h: (0, 0, 0, 0)),
        ],
        out_specs=pl.BlockSpec((2, per, chans, bins), lambda r, h: (0, r * blocks + h, 0, 0)),
        scratch_shapes=[
            pltpu.VMEM((chans, 2 * wins, bins), f32),
            pltpu.VMEM((2, wins, chans, bins), bf16),
        ],
        name="cross",
    )(offset, src, loc)


def chip_grid(size):
    chips = size // 2
    cols = 1
    while cols * cols * 4 <= chips:
        cols *= 2
    return chips // cols, cols


HOP = 6


def build_bank(bank_ref, toep):
    _, nbank, ntap = bank_ref.shape
    outs = toep.shape[1] // (2 * nbank)
    for b in range(nbank):
        parts = []
        for p in range(2):
            row = jnp.concatenate(
                [bank_ref[p, b : b + 1, :], jnp.zeros((1, LANES - ntap), f32)], axis=1
            )
            full = jnp.broadcast_to(row, (outs, LANES))
            parts.append(split(pltpu.roll(full, 0, 1, stride=1, stride_axis=0)))
        at = b * 2 * outs
        for part in range(2):
            real, imag = parts[0][part], parts[1][part]
            toep[part, at : at + outs, :LANES] = real
            toep[part, at : at + outs, LANES:] = -imag
            toep[part, at + outs : at + 2 * outs, :LANES] = imag
            toep[part, at + outs : at + 2 * outs, LANES:] = real


def build_band(band):
    wide, bins = band.shape
    rows = lax.broadcasted_iota(jnp.int32, (wide, bins), 0)
    cols = lax.broadcasted_iota(jnp.int32, (wide, bins), 1)
    band[...] = (jnp.abs(rows - bins - cols) <= SMOOTH // 2).astype(f32).astype(bf16)


def build_pick(base, place, owner_ref, offset_ref, masks, pick):
    parts, _, chans = masks.shape
    rounds = offset_ref.shape[0]
    total = parts * chans
    valid = jnp.concatenate(
        [masks[b, pl.ds(place, 1), :].astype(f32) for b in range(parts)], axis=1
    )
    eye = lax.broadcasted_iota(jnp.int32, (chans, chans), 0) == lax.broadcasted_iota(
        jnp.int32, (chans, chans), 1
    )
    cols = lax.broadcasted_iota(jnp.int32, (chans, total), 1).astype(f32)
    for r in range(rounds):
        row = jnp.broadcast_to(offset_ref[r : r + 1, :].astype(f32), (chans, chans))
        col = jnp.sum(jnp.where(eye, row, 0.0), axis=1, keepdims=True)
        col = col + ((owner_ref[r] - base) * chans).astype(f32)
        pick[r * chans : (r + 1) * chans] = jnp.where(cols == col, valid, 0.0).astype(bf16)
    rows = lax.broadcasted_iota(jnp.int32, (total, total), 0)
    same = rows == lax.broadcasted_iota(jnp.int32, (total, total), 1)
    pick[rounds * chans :] = jnp.where(same, valid, 0.0).astype(bf16)


def filter_cut(q, nbank, raw, toep, index_ref, filt, power):
    outs = toep.shape[1] // (2 * nbank)
    blocks, chans = raw.shape[1], raw.shape[3]
    step = outs // chans
    index = index_ref[:, q * LANES : (q + 1) * LANES]
    for u in range((blocks - 2) // step):
        here = [
            raw[q, u * step : u * step + step + 2, p].reshape((step + 2) * chans, LANES)
            for p in range(2)
        ]
        here = jnp.concatenate(here, axis=0)
        res = jnp.dot(toep[0], here, preferred_element_type=f32)
        res += jnp.dot(toep[1], here, preferred_element_type=f32)
        acc = res[: 2 * outs]
        for b in range(1, nbank):
            acc = jnp.where(index == b, res[2 * outs * b : 2 * outs * (b + 1)], acc)
        real, imag = acc[:outs], acc[outs:]
        rows = slice(u * outs, (u + 1) * outs)
        filt[q, 0, rows] = real
        filt[q, 1, rows] = imag
        power[rows, (q + 1) * LANES : (q + 2) * LANES] = (real * real + imag * imag).astype(bf16)


def whiten_cut(q, band, pick, filt, power, own, mine):
    rounds = own.shape[0] // filt.shape[0]
    chans = own.shape[2]
    smooth = jnp.dot(
        power[:, q * LANES : (q + 3) * LANES], band[...], preferred_element_type=f32
    )
    scale = lax.rsqrt(smooth * (1.0 / SMOOTH) + water_level)
    for p in range(2):
        white = (filt[q, p] * scale).astype(bf16)
        res = jnp.dot(pick[...], white, preferred_element_type=f32).astype(bf16)
        for r in range(rounds):
            own[q * rounds + r, p] = res[r * chans : (r + 1) * chans]
        at = rounds * chans
        for b in range(mine.shape[1]):
            mine[q, b, p] = res[at + b * chans : at + (b + 1) * chans]


def row_kernel(
    rows,
    owner_in,
    own_in,
    bank_in,
    index_in,
    mask_in,
    offset_in,
    loc_ref,
    src_ref,
    owner_ref,
    own_ref,
    bank_ref,
    index_ref,
    mask_ref,
    offset_ref,
    in_sems,
    raw,
    masks,
    toep,
    band,
    pick,
    filt,
    power,
    mine,
    back,
    line_buf,
    done,
    across,
    beside,
    raw_send,
    raw_recv,
    mask_sems,
    back_sems,
    line_sems,
    give_sems,
):
    wins, chans = mask_ref.shape
    cuts = raw.shape[0]
    nbank = bank_ref.shape[1]
    parts = wins
    rounds = owner_ref.shape[0]
    me = lax.axis_index("chan")
    core = me % 2
    place = me % parts
    base = me - place
    row = me // parts
    partner = me + 1 - 2 * core
    alike = base + (place + 2) % parts
    partner_place = place + 1 - 2 * core
    alike_place = (place + 2) % parts
    corner_place = (partner_place + 2) % parts
    mesh_id = pl.DeviceIdType.MESH

    def send(src, dst, send_sem, recv_sem, who):
        return pltpu.make_async_remote_copy(
            src_ref=src,
            dst_ref=dst,
            send_sem=send_sem,
            recv_sem=recv_sem,
            device_id={"chan": who},
            device_id_type=mesh_id,
        )

    pairs_in = [
        (own_in, own_ref),
        (mask_in, mask_ref),
        (bank_in, bank_ref),
        (index_in, index_ref),
        (offset_in, offset_ref),
        (owner_in, owner_ref),
    ]
    inputs = [
        pltpu.make_async_copy(src, dst, in_sems.at[n]) for n, (src, dst) in enumerate(pairs_in)
    ]
    for copy in inputs:
        copy.start()

    barrier = pltpu.get_barrier_semaphore()
    partners = [(place != j, base + j) for j in range(parts)]
    for j in range(parts):
        near = jnp.logical_or(place == j, jnp.logical_or(place == parts - 1, j == 0))
        partners.append((jnp.logical_and(row < rows - 1, near), base + parts + j))
        near = jnp.logical_or(place == j, jnp.logical_or(place == 0, j == parts - 1))
        partners.append((jnp.logical_and(row > 0, near), base - parts + j))
    expected = jnp.int32(0)
    for there, who in partners:
        expected += there.astype(jnp.int32)

        @pl.when(there)
        def _(who=who):
            pl.semaphore_signal(barrier, inc=1, device_id={"chan": who}, device_id_type=mesh_id)

    pl.semaphore_wait(barrier, expected)

    peers = [alike_place, corner_place, partner_place]

    def raw_copy(q, to, slot, n, who):
        return send(
            own_ref.at[:, to, :, q * LANES : (q + 1) * LANES],
            raw.at[q, slot],
            raw_send.at[q, n],
            raw_recv.at[q, slot],
            who,
        )

    def mask_copy(n):
        return send(
            mask_ref, masks.at[place], mask_sems.at[0, n], mask_sems.at[1, place], base + peers[n]
        )

    above = jnp.logical_and(place == parts - 1, row < rows - 1)
    below = jnp.logical_and(place == 0, row > 0)

    def edges(q, act):
        @pl.when(above)
        def _():
            for j in range(parts):
                act(raw_copy(q, j, 0, parts - 1 + j, base + parts + j))

        @pl.when(below)
        def _():
            for j in range(parts):
                act(raw_copy(q, j, parts + 1, parts - 1 + j, base - parts + j))

    for copy in inputs:
        copy.wait()
    for n in range(parts - 1):
        mask_copy(n).start()
    for q in range(cuts):
        for n in range(2):
            raw_copy(q, peers[n], 1 + place, n, base + peers[n]).start()
        edges(q, lambda copy: copy.start())
        raw_copy(q, peers[2], 1 + place, 2, base + peers[2]).start()

    masks[place] = mask_ref[...]
    for q in range(cuts):
        raw[q, 1 + place] = own_ref[:, place, :, q * LANES : (q + 1) * LANES]

    @pl.when(row == 0)
    def _():
        raw[:, 0] = jnp.zeros_like(raw[:, 0])

    @pl.when(row == rows - 1)
    def _():
        raw[:, parts + 1] = jnp.zeros_like(raw[:, parts + 1])

    line = Line(row, rows, lambda i: i * parts + place, HOP, (*line_buf, line_sems))
    line.clear()
    build_bank(bank_ref, toep)
    build_band(band)
    edge = jnp.zeros((power.shape[0], LANES), bf16)
    power[:, :LANES] = edge
    power[:, (cuts + 1) * LANES :] = edge

    for b in range(parts):

        @pl.when(place != b)
        def _(b=b):
            send(mask_ref, masks.at[b], mask_sems.at[0, 0], mask_sems.at[1, b], partner).wait_recv()

    build_pick(base, place, owner_ref, offset_ref, masks, pick)

    count = line.count
    last = HOP * (rows - 1)

    def give(src, dst, n, k, who):
        return send(src.at[k], dst.at[k], give_sems.at[0, n, k], give_sems.at[1, n, k], who)

    def put(k, j, value):
        src_ref[k, j] = value.astype(f32) * (1.0 / wins)

    def tick(t):
        line.tick(t)
        k = t - last

        @pl.when(jnp.logical_and(k >= 0, k < count))
        def _():
            total = line.result(k)
            done[k] = total
            give(done, across, 0, k, alike).start()
            give(done, beside.at[0], 1, k, partner).start()
            put(k, place, total)

        q = t - last - HOP

        @pl.when(jnp.logical_and(q >= 0, q < count))
        def _():
            give(done, across, 0, q, alike).wait_recv()
            give(across, beside.at[1], 2, q, partner).start()
            put(q, alike_place, across[q])

        b = t - last - 2 * HOP

        @pl.when(jnp.logical_and(b >= 0, b < count))
        def _():
            give(done, beside.at[0], 1, b, partner).wait_recv()
            put(b, partner_place, beside[0, b])
            give(across, beside.at[1], 2, b, partner).wait_recv()
            put(b, corner_place, beside[1, b])

    def back_copy(q, n):
        return send(
            mine.at[q, peers[n]],
            back.at[q, place],
            back_sems.at[0, q, n],
            back_sems.at[1, q, place],
            base + peers[n],
        )

    def finish(q):
        whiten_cut(q, band, pick, filt, power, line.own, mine)
        back[q, place] = mine[q, place]

        @pl.loop(q * rounds, (q + 1) * rounds)
        def _(t):
            tick(t)

        for n in range(parts - 1):
            back_copy(q, n).start()

    for q in range(cuts):
        for slot in range(parts + 2):
            there = place != slot - 1
            if slot == 0:
                there = row > 0
            if slot == parts + 1:
                there = row < rows - 1

            @pl.when(there)
            def _(slot=slot, q=q):
                raw_copy(q, 0, slot, 0, partner).wait_recv()

        filter_cut(q, nbank, raw, toep, index_ref, filt, power)
        if q > 0:
            finish(q - 1)
    finish(cuts - 1)

    @pl.loop(cuts * rounds, count + last + 2 * HOP)
    def _(t):
        tick(t)

    for q in range(cuts):
        for n in range(parts - 1):
            j = peers[n]
            send(
                mine.at[q, 0], back.at[q, j], back_sems.at[0, q, n], back_sems.at[1, q, j], partner
            ).wait_recv()
    loc_ref[...] = back[...]

    for n in range(parts - 1):
        mask_copy(n).wait_send()
    for q in range(cuts):
        for n in range(parts - 1):
            raw_copy(q, peers[n], 1 + place, n, base + peers[n]).wait_send()
            back_copy(q, n).wait_send()
        edges(q, lambda copy: copy.wait_send())
    line.drain()

    @pl.loop(0, count)
    def _(k):
        give(done, across, 0, k, alike).wait_send()
        give(done, beside.at[0], 1, k, partner).wait_send()
        give(across, beside.at[1], 2, k, partner).wait_send()


def row_front(rows, owner, own, bank, index, mask, offset):
    _, wins, chans, bins = own.shape
    nbank = bank.shape[1]
    rounds = owner.shape[0]
    cuts = bins // LANES
    parts = wins
    count = cuts * rounds
    outs = LANES // 2
    vmem = pl.BlockSpec(memory_space=pltpu.VMEM)
    chunk = (2, chans, LANES)
    chunks = pltpu.VMEM((count, *chunk), bf16)
    return pl.pallas_call(
        functools.partial(row_kernel, rows),
        out_shape=[
            jax.ShapeDtypeStruct((cuts, wins, *chunk), bf16),
            jax.ShapeDtypeStruct((count, wins, *chunk), f32),
        ],
        in_specs=[pl.BlockSpec(memory_space=pltpu.HBM)] * 6,
        out_specs=[vmem] * 2,
        scratch_shapes=[
            pltpu.SMEM(owner.shape, owner.dtype),
            *[pltpu.VMEM(a.shape, a.dtype) for a in (own, bank, index, mask, offset)],
            pltpu.SemaphoreType.DMA((6,)),
            pltpu.VMEM((cuts, parts + 2, *chunk), bf16),
            pltpu.VMEM((parts, wins, chans), jnp.int32),
            pltpu.VMEM((2, nbank * 2 * outs, 2 * LANES), bf16),
            pltpu.VMEM((3 * LANES, LANES), bf16),
            pltpu.VMEM(((rounds + parts) * chans, parts * chans), bf16),
            pltpu.VMEM((cuts, 2, parts * chans, LANES), f32),
            pltpu.VMEM((parts * chans, (cuts + 2) * LANES), bf16),
            pltpu.VMEM((cuts, parts, *chunk), bf16),
            pltpu.VMEM((cuts, parts, *chunk), bf16),
            [chunks] * 5,
            chunks,
            chunks,
            pltpu.VMEM((2, count, *chunk), bf16),
            pltpu.SemaphoreType.DMA((cuts, 2 * parts - 1)),
            pltpu.SemaphoreType.DMA((cuts, parts + 2)),
            pltpu.SemaphoreType.DMA((2, parts)),
            pltpu.SemaphoreType.DMA((2, cuts, parts)),
            pltpu.SemaphoreType.DMA((2, 2, count)),
            pltpu.SemaphoreType.DMA((2, 3, count)),
        ],
        compiler_params=pltpu.CompilerParams(
            collective_id=0, has_side_effects=True, vmem_limit_bytes=24 << 20
        ),
        name="front",
    )(*[pltpu.with_memory_space_constraint(a, pltpu.HBM) for a in (owner, own, bank, index, mask, offset)])


def pairs_kernel(src_ref, loc_ref, out_ref, buf, sems):
    cuts, wins, _, chans, _ = loc_ref.shape
    slots, _, per = buf.shape[:3]
    rounds = src_ref.shape[0] // cuts
    steps = rounds * chans // per

    def flush(step):
        slot = step % slots
        return pltpu.make_async_copy(
            buf.at[slot], out_ref.at[:, pl.ds(step * per, per)], sems.at[slot]
        )

    @pl.loop(0, steps)
    def _(step):
        slot = step % slots
        r = step * per // chans
        first = step * per % chans

        @pl.when(step >= slots)
        def _():
            flush(step - slots).wait()

        for q in range(cuts):
            loc = [[loc_ref[q, w, p] for w in range(wins)] for p in range(2)]

            def one(j, carry, q=q, loc=loc):
                src = [
                    [
                        jnp.broadcast_to(
                            src_ref[q * rounds + r, w, p, pl.ds(first + j, 1), :], (chans, LANES)
                        ).astype(bf16)
                        for w in range(wins)
                    ]
                    for p in range(2)
                ]
                real = tree_sum([src[p][w] * loc[p][w] for w in range(wins) for p in range(2)])
                plus = tree_sum([src[0][w] * loc[1][w] for w in range(wins)])
                minus = tree_sum([src[1][w] * loc[0][w] for w in range(wins)])
                cut = slice(q * LANES, (q + 1) * LANES)
                buf[slot, 0, j, :, cut] = real
                buf[slot, 1, j, :, cut] = plus - minus
                return carry

            lax.fori_loop(0, per, one, 0, unroll=8)
        flush(step).start()

    for n in range(slots):
        flush(steps - slots + n).wait()


def pairs(src, loc):
    cuts, wins, _, chans, _ = loc.shape
    count = src.shape[0] // cuts * chans
    per = chans // 2
    slots = 2
    vmem = pl.BlockSpec(memory_space=pltpu.VMEM)
    return pl.pallas_call(
        pairs_kernel,
        out_shape=jax.ShapeDtypeStruct((2, count, chans, cuts * LANES), bf16),
        in_specs=[vmem] * 2,
        out_specs=pl.BlockSpec(memory_space=pl.ANY),
        scratch_shapes=[
            pltpu.VMEM((slots, 2, per, chans, cuts * LANES), bf16),
            pltpu.SemaphoreType.DMA((slots,)),
        ],
        compiler_params=pltpu.CompilerParams(vmem_limit_bytes=16 << 20),
        name="pairs",
    )(src, loc)


def body(spectra, filter_bank, band_index, window_mask, owner_order, source_offset):
    grid = chip_grid(lax.axis_size("chan"))
    _, wins, chans, bins = spectra.shape
    ntap = filter_bank.shape[2]
    if 2 * grid[1] == wins == 4 and 4 * chans == LANES and ntap == 2 * chans + 1:
        whitened, sources = row_front(
            grid[0],
            owner_order,
            spectra,
            filter_bank,
            band_index[None, :],
            window_mask,
            source_offset,
        )
        return pairs(sources, whitened)
    whitened, sources = front(
        grid, owner_order, spectra, filter_bank, band_index[None, :], window_mask
    )
    sources = sources.reshape(sources.shape[0], wins, 2, chans, bins)
    return cross(source_offset, sources, whitened)


def solution(mesh):
    in_specs = (
        P(None, "groups", "chan", None),
        P(),
        P(),
        P("groups", "chan"),
        P("groups"),
        P("groups", None),
    )
    out_specs = P(None, "groups", "chan", None)
    return jax.shard_map(body, mesh=mesh, in_specs=in_specs, out_specs=out_specs, check_vma=False)
```

```python
import functools

import jax
import jax.numpy as jnp
from jax import lax
from jax.experimental import pallas as pl
from jax.experimental.pallas import tpu as pltpu
from jax.sharding import PartitionSpec as P

SMOOTH = 17
water_level = 0.05
bf16 = jnp.bfloat16
f32 = jnp.float32
LANES = 128
LAG = 4


def split(x):
    hi = x.astype(bf16)
    return hi, (x - hi.astype(f32)).astype(bf16)


def build_toeplitz(bank_ref, toep):
    _, nbank, ntap = bank_ref.shape
    chans = toep.shape[1] // (2 * nbank)
    for b in range(nbank):
        parts = []
        for p in range(2):
            row = jnp.concatenate(
                [bank_ref[p, b : b + 1, :], jnp.zeros((1, LANES - ntap), f32)], axis=1
            )
            full = jnp.broadcast_to(row, (chans, LANES))
            parts.append(split(pltpu.roll(full, 0, 1, stride=1, stride_axis=0)))
        at = b * 2 * chans
        for part in range(2):
            real, imag = parts[0][part], parts[1][part]
            toep[part, at : at + chans, :LANES] = real
            toep[part, at : at + chans, LANES:] = -imag
            toep[part, at + chans : at + 2 * chans, :LANES] = imag
            toep[part, at + chans : at + 2 * chans, LANES:] = real


def build_window(band):
    bins = band.shape[0]
    rows = lax.broadcasted_iota(jnp.int32, (bins, bins), 0)
    cols = lax.broadcasted_iota(jnp.int32, (bins, bins), 1)
    band[...] = (jnp.abs(rows - cols) <= SMOOTH // 2).astype(f32).astype(bf16)


def filter_window(nbank, w, x, toep, index_ref, filt, power):
    bins = filt.shape[2]
    chans = toep.shape[1] // (2 * nbank)
    tile = 256
    rows = slice(w * chans, (w + 1) * chans)
    for n in range(bins // tile):
        cut = slice(n * tile, (n + 1) * tile)
        here = x(cut)
        res = jnp.dot(toep[0], here, preferred_element_type=f32)
        res += jnp.dot(toep[1], here, preferred_element_type=f32)
        index = index_ref[:, cut]
        acc = res[: 2 * chans]
        for b in range(1, nbank):
            acc = jnp.where(index == b, res[2 * chans * b : 2 * chans * (b + 1)], acc)
        real, imag = acc[:chans], acc[chans:]
        filt[0, rows, cut] = real
        filt[1, rows, cut] = imag
        hi, lo = split(real * real + imag * imag)
        power[0, rows, cut] = hi
        power[1, rows, cut] = lo


def whiten_window(w, band, mask_ref, filt, power):
    chans = mask_ref.shape[1]
    rows = slice(w * chans, (w + 1) * chans)
    smooth = jnp.dot(power[0, rows], band[...], preferred_element_type=f32)
    smooth += jnp.dot(power[1, rows], band[...], preferred_element_type=f32)
    scale = lax.rsqrt(smooth * (1.0 / SMOOTH) + water_level)
    eye = lax.broadcasted_iota(jnp.int32, (chans, chans), 0) == lax.broadcasted_iota(
        jnp.int32, (chans, chans), 1
    )
    row = jnp.broadcast_to(mask_ref[w : w + 1, :].astype(f32), (chans, chans))
    valid = jnp.sum(jnp.where(eye, row, 0.0), axis=1, keepdims=True)
    scale = scale * valid
    return [(filt[p, rows] * scale).astype(bf16) for p in range(2)]


class Line:
    def __init__(self, pos, length, device_of, lag, refs):
        self.pos, self.length, self.device_of, self.lag = pos, length, device_of, lag
        self.own, self.out_r, self.out_l, self.in_r, self.in_l, self.sems = refs
        self.count = self.own.shape[0]

    def clear(self):
        @pl.when(self.pos == 0)
        def _():
            self.in_r[...] = jnp.zeros_like(self.in_r)

        @pl.when(self.pos == self.length - 1)
        def _():
            self.in_l[...] = jnp.zeros_like(self.in_l)

    def copy(self, way, k):
        out, into = (self.out_r, self.in_r) if way == 0 else (self.out_l, self.in_l)
        other = self.pos + 1 if way == 0 else self.pos - 1
        return pltpu.make_async_remote_copy(
            src_ref=out.at[k],
            dst_ref=into.at[k],
            send_sem=self.sems.at[way, 0, k],
            recv_sem=self.sems.at[way, 1, k],
            device_id={"chan": self.device_of(other)},
            device_id_type=pl.DeviceIdType.MESH,
        )

    def tick(self, t):
        for way in range(2):
            behind = self.pos if way == 0 else self.length - 1 - self.pos
            out, into = (self.out_r, self.in_r) if way == 0 else (self.out_l, self.in_l)
            k = t - self.lag * behind
            inside = jnp.logical_and(k >= 0, k < self.count)

            @pl.when(jnp.logical_and(inside, behind > 0))
            def _(way=way, k=k):
                self.copy(way, k).wait_recv()

            @pl.when(jnp.logical_and(inside, behind < self.length - 1))
            def _(way=way, k=k, out=out, into=into):
                out[k] = self.own[k] + into[k]
                self.copy(way, k).start()

    def result(self, k):
        return self.own[k] + self.in_r[k] + self.in_l[k]

    def drain(self):
        for way in range(2):
            behind = self.pos if way == 0 else self.length - 1 - self.pos

            @pl.when(behind < self.length - 1)
            def _(way=way):
                @pl.loop(0, self.count)
                def _(k):
                    self.copy(way, k).wait_send()


def front_kernel(
    rows,
    cols,
    owner_ref,
    own_ref,
    bank_ref,
    index_ref,
    mask_ref,
    out_ref,
    src_ref,
    halo,
    toep,
    band,
    filt,
    power,
    mine,
    beside,
    row_buf,
    done,
    gathered,
    halo_sems,
    beside_sems,
    row_sems,
    gather_sems,
):
    wins, chans = mask_ref.shape
    bins = own_ref.shape[3]
    parts = 2 * cols
    subs, piece = beside.shape[1], beside.shape[2]
    me = lax.axis_index("chan")
    size = rows * cols * 2
    core = me % 2
    place = me % (2 * cols)
    base = me - place
    row = me // (2 * cols)
    partner = me + 1 - 2 * core
    mesh_id = pl.DeviceIdType.MESH

    barrier = pltpu.get_barrier_semaphore()
    partners = [
        (me > 0, me - 1),
        (me < size - 1, me + 1),
        (row > 0, me - 2 * cols),
        (row < rows - 1, me + 2 * cols),
    ] + [(place != j, base + j) for j in range(2 * cols)]
    expected = jnp.int32(0)
    for there, who in partners:
        expected += there.astype(jnp.int32)

        @pl.when(there)
        def _(who=who):
            pl.semaphore_signal(barrier, inc=1, device_id={"chan": who}, device_id_type=mesh_id)

    pl.semaphore_wait(barrier, expected)

    def halo_copy(way, w):
        return pltpu.make_async_remote_copy(
            src_ref=own_ref.at[:, w],
            dst_ref=halo.at[way, :, w],
            send_sem=halo_sems.at[way, 0, w],
            recv_sem=halo_sems.at[way, 1, w],
            device_id={"chan": me + 1 - 2 * way},
            device_id_type=mesh_id,
        )

    order = list(range(wins))
    sends = (me < size - 1, me > 0)
    for w in order:
        for way in range(2):

            @pl.when(sends[way])
            def _(way=way, w=w):
                halo_copy(way, w).start()

    for way in range(2):

        @pl.when(jnp.logical_not(sends[1 - way]))
        def _(way=way):
            halo[way] = jnp.zeros_like(halo[way])

    line = Line(row, rows, lambda i: i * 2 * cols + place, LAG, (*row_buf, row_sems))
    line.clear()
    build_toeplitz(bank_ref, toep)
    build_window(band)

    def beside_copy(sender, j):
        return pltpu.make_async_remote_copy(
            src_ref=mine.at[pl.ds(j * subs, subs)],
            dst_ref=beside.at[sender],
            send_sem=beside_sems.at[0, j],
            recv_sem=beside_sems.at[1, sender],
            device_id={"chan": base + j},
            device_id_type=mesh_id,
        )

    blank = jnp.zeros((LANES - 3 * chans, bins), bf16)
    for w in order:
        for way in range(2):

            @pl.when(sends[1 - way])
            def _(way=way, w=w):
                halo_copy(way, w).wait_recv()

        def x(cut, w=w):
            stack = []
            for p in range(2):
                stack += [halo[0, p, w, :, cut], own_ref[p, w, :, cut], halo[1, p, w, :, cut]]
                stack += [blank[:, cut]]
            return jnp.concatenate(stack, axis=0)

        filter_window(bank_ref.shape[1], w, x, toep, index_ref, filt, power)
        white = whiten_window(w, band, mask_ref, filt, power)
        for p in range(2):
            out_ref[p, w] = white[p]
            for i in range(chans // piece):
                mine[(w * 2 + p) * (chans // piece) + i] = white[p][i * piece : (i + 1) * piece]
        for j in range(w * parts // wins, (w + 1) * parts // wins):

            @pl.when(place != j)
            def _(j=j):
                beside_copy(place, j).start()

    beside[place] = mine[pl.ds(place * subs, subs)]
    for j in range(parts):

        @pl.when(place != j)
        def _(j=j):
            beside_copy(j, j).wait_recv()

    count = line.count

    @pl.loop(0, count)
    def _(k):
        total = jnp.zeros((piece, bins), bf16)
        for j in range(parts):
            total += beside[j, k % subs] * (owner_ref[k // subs] == base + j).astype(f32).astype(bf16)
        line.own[k] = total

    def give(src, origin, k, sem, who):
        return pltpu.make_async_remote_copy(
            src_ref=src,
            dst_ref=gathered.at[origin, k],
            send_sem=gather_sems.at[sem, k],
            recv_sem=gather_sems.at[2 * parts + origin, k],
            device_id={"chan": who},
            device_id_type=mesh_id,
        )

    def put(j, k, value):
        src_ref[k // subs, j * subs + k % subs] = value

    alike = [jnp.logical_and(place != j, core == j % 2) for j in range(parts)]
    last = LAG * (rows - 1)

    @pl.loop(0, count + last + LAG)
    def _(t):
        line.tick(t)
        k = t - last

        @pl.when(jnp.logical_and(k >= 0, k < count))
        def _():
            total = line.result(k)
            done[k] = total
            for j in range(parts):

                @pl.when(alike[j])
                def _(j=j):
                    give(done.at[k], place, k, j, base + j).start()

            give(done.at[k], place, k, parts + place, partner).start()
            put(place, k, total)

        q = t - last - LAG

        @pl.when(q >= 0)
        def _():
            for j in range(parts):

                @pl.when(alike[j])
                def _(j=j):
                    give(done.at[q], j, q, j, partner).wait_recv()
                    give(gathered.at[j, q], j, q, parts + j, partner).start()
                    put(j, q, gathered[j, q])

    @pl.loop(0, count)
    def _(k):
        for j in range(parts):

            @pl.when(core != j % 2)
            def _(j=j):
                give(done.at[k], j, k, j, partner).wait_recv()
                put(j, k, gathered[j, k])

    for way in range(2):
        for w in range(wins):

            @pl.when(sends[way])
            def _(way=way, w=w):
                halo_copy(way, w).wait_send()

    for j in range(parts):

        @pl.when(place != j)
        def _(j=j):
            beside_copy(place, j).wait_send()

    line.drain()

    @pl.loop(0, count)
    def _(k):
        give(done.at[k], place, k, parts + place, partner).wait_send()
        for j in range(parts):

            @pl.when(alike[j])
            def _(j=j):
                give(done.at[k], place, k, j, partner).wait_send()
                give(gathered.at[j, k], j, k, parts + j, partner).wait_send()


def front(grid, owner, own, bank, index, mask):
    _, wins, chans, bins = own.shape
    nbank = bank.shape[1]
    rounds = owner.shape[0]
    rows, cols = grid
    parts = 2 * cols
    total = wins * 2 * chans
    piece = min(chans, total // parts)
    subs = total // parts // piece
    count = rounds * subs
    vmem = pl.BlockSpec(memory_space=pltpu.VMEM)
    chunk = (piece, bins)
    chunks = pltpu.VMEM((count, *chunk), bf16)
    return pl.pallas_call(
        functools.partial(front_kernel, rows, cols),
        out_shape=[
            jax.ShapeDtypeStruct(own.shape, bf16),
            jax.ShapeDtypeStruct((rounds, parts * subs, piece, bins), bf16),
        ],
        in_specs=[pl.BlockSpec(memory_space=pltpu.SMEM)] + [vmem] * 4,
        out_specs=[vmem] * 2,
        scratch_shapes=[
            pltpu.VMEM((2, *own.shape), bf16),
            pltpu.VMEM((2, nbank * 2 * chans, 2 * LANES), bf16),
            pltpu.VMEM((bins, bins), bf16),
            pltpu.VMEM((2, wins * chans, bins), f32),
            pltpu.VMEM((2, wins * chans, bins), bf16),
            pltpu.VMEM((parts * subs, *chunk), bf16),
            pltpu.VMEM((parts, subs, *chunk), bf16),
            [chunks] * 5,
            chunks,
            pltpu.VMEM((parts, count, *chunk), bf16),
            pltpu.SemaphoreType.DMA((2, 2, wins)),
            pltpu.SemaphoreType.DMA((2, parts)),
            pltpu.SemaphoreType.DMA((2, 2, count)),
            pltpu.SemaphoreType.DMA((3 * parts, count)),
        ],
        compiler_params=pltpu.CompilerParams(collective_id=0, has_side_effects=True),
        name="front",
    )(owner, own, bank, index, mask)


def tree_sum(terms):
    while len(terms) > 1:
        terms = [a + b for a, b in zip(terms[::2], terms[1::2])]
    return terms[0]


def cross_kernel(offset_ref, src_ref, loc_ref, out_ref, wide, held):
    _, wins, chans, bins = loc_ref.shape
    count = out_ref.shape[1]
    r, h = pl.program_id(0), pl.program_id(1)

    @pl.when(jnp.logical_and(r == 0, h == 0))
    def _():
        held[...] = loc_ref[...]

    @pl.when(h == 0)
    def _():
        for p in range(2):
            for w in range(wins):
                wide[:, p * wins + w, :] = src_ref[0, w, p].astype(f32) * (1.0 / wins)

    for n in range(bins // LANES):
        cut = slice(n * LANES, (n + 1) * LANES)

        def one(j, carry, cut=cut):
            loc = [[held[p, w, :, cut] for w in range(wins)] for p in range(2)]
            at = offset_ref[r, h * count + j]
            src = [
                [
                    jnp.broadcast_to(
                        wide[at, p * wins + w : p * wins + w + 1, cut], (chans, LANES)
                    ).astype(bf16)
                    for w in range(wins)
                ]
                for p in range(2)
            ]
            real = tree_sum(
                [src[p][w] * loc[p][w] for w in range(wins) for p in range(2)]
            )
            plus = tree_sum([src[0][w] * loc[1][w] for w in range(wins)])
            minus = tree_sum([src[1][w] * loc[0][w] for w in range(wins)])
            out_ref[0, j, :, cut] = real
            out_ref[1, j, :, cut] = plus - minus
            return carry

        lax.fori_loop(0, count, one, 0, unroll=4)


def cross(offset, src, loc, blocks=1):
    rounds, wins, _, chans, bins = src.shape
    per = chans // blocks
    return pl.pallas_call(
        cross_kernel,
        out_shape=jax.ShapeDtypeStruct((2, rounds * chans, chans, bins), bf16),
        grid=(rounds, blocks),
        in_specs=[
            pl.BlockSpec(memory_space=pltpu.SMEM),
            pl.BlockSpec((1, wins, 2, chans, bins), lambda r, h: (r, 0, 0, 0, 0)),
            pl.BlockSpec((2, wins, chans, bins), lambda r, h: (0, 0, 0, 0)),
        ],
        out_specs=pl.BlockSpec((2, per, chans, bins), lambda r, h: (0, r * blocks + h, 0, 0)),
        scratch_shapes=[
            pltpu.VMEM((chans, 2 * wins, bins), f32),
            pltpu.VMEM((2, wins, chans, bins), bf16),
        ],
        name="cross",
    )(offset, src, loc)


def chip_grid(size):
    chips = size // 2
    cols = 1
    while cols * cols * 4 <= chips:
        cols *= 2
    return chips // cols, cols


HOP, SIDE, NEAR = 10, 8, 4


class Chain(Line):
    def copy(self, way, k):
        out, into = (self.out_r, self.in_r) if way == 0 else (self.out_l, self.in_l)
        other = self.pos + 1 if way == 0 else self.pos - 1
        return self.make(way, out.at[k], into.at[k], k, self.device_of(other))

    def make(self, way, src, dst, k, who):
        return pltpu.make_async_remote_copy(
            src_ref=src,
            dst_ref=dst,
            send_sem=self.sems.at[way, self.count],
            recv_sem=self.sems.at[way, k],
            device_id={"chan": who},
            device_id_type=pl.DeviceIdType.MESH,
        )

    def drain(self, who):
        for way in range(2):
            behind = self.pos if way == 0 else self.length - 1 - self.pos
            out = self.out_r if way == 0 else self.out_l

            @pl.when(behind < self.length - 1)
            def _(way=way, out=out):
                self.make(way, out, out, 0, who).wait_send()


def build_bank(bank_ref, toep):
    _, nbank, ntap = bank_ref.shape
    outs = toep.shape[0] // (2 * nbank)
    for b in range(nbank):
        parts = []
        for p in range(2):
            row = jnp.concatenate(
                [bank_ref[p, b : b + 1, :], jnp.zeros((1, LANES - ntap), f32)], axis=1
            )
            full = jnp.broadcast_to(row, (outs, LANES))
            parts.append(split(pltpu.roll(full, 0, 1, stride=1, stride_axis=0)))
        at = b * 2 * outs
        for part in range(2):
            real, imag = parts[0][part], parts[1][part]
            left = slice(2 * part * LANES, (2 * part + 1) * LANES)
            right = slice((2 * part + 1) * LANES, (2 * part + 2) * LANES)
            toep[at : at + outs, left] = real
            toep[at : at + outs, right] = -imag
            toep[at + outs : at + 2 * outs, left] = imag
            toep[at + outs : at + 2 * outs, right] = real


def build_band(band):
    wide, bins = band.shape
    rows = lax.broadcasted_iota(jnp.int32, (wide, bins), 0)
    cols = lax.broadcasted_iota(jnp.int32, (wide, bins), 1)
    band[...] = (jnp.abs(rows - bins - cols) <= SMOOTH // 2).astype(f32).astype(bf16)


def build_pick(base, place, owner_ref, offset_ref, masks, pick):
    parts, _, chans = masks.shape
    rounds = offset_ref.shape[0]
    total = parts * chans
    valid = jnp.concatenate(
        [masks[b, pl.ds(place, 1), :].astype(f32) for b in range(parts)], axis=1
    )
    eye = lax.broadcasted_iota(jnp.int32, (chans, chans), 0) == lax.broadcasted_iota(
        jnp.int32, (chans, chans), 1
    )
    cols = lax.broadcasted_iota(jnp.int32, (chans, total), 1).astype(f32)
    for r in range(rounds):
        row = jnp.broadcast_to(offset_ref[r : r + 1, :].astype(f32), (chans, chans))
        col = jnp.sum(jnp.where(eye, row, 0.0), axis=1, keepdims=True)
        col = col + ((owner_ref[r] - base) * chans).astype(f32)
        pick[r * chans : (r + 1) * chans] = jnp.where(cols == col, valid, 0.0).astype(bf16)
    rows = lax.broadcasted_iota(jnp.int32, (total, total), 0)
    same = rows == lax.broadcasted_iota(jnp.int32, (total, total), 1)
    pick[rounds * chans :] = jnp.where(same, valid, 0.0).astype(bf16)


def filter_cuts(first, cuts, nbank, raw, toep, index_ref, filt, power):
    outs = toep.shape[0] // (2 * nbank)
    blocks, chans = raw.shape[1], raw.shape[3]
    step = outs // chans
    many = range(first, first + cuts)
    index = index_ref[:, first * LANES : (first + cuts) * LANES]
    for u in range((blocks - 2) // step):
        here = [
            jnp.concatenate(
                [
                    raw[q, u * step : u * step + step + 2, p].reshape((step + 2) * chans, LANES)
                    for q in many
                ],
                axis=1,
            )
            for p in range(2)
        ]
        res = jnp.dot(
            toep[...], jnp.concatenate(here + here, axis=0), preferred_element_type=f32
        )
        acc = res[: 2 * outs]
        for b in range(1, nbank):
            acc = jnp.where(index == b, res[2 * outs * b : 2 * outs * (b + 1)], acc)
        real, imag = acc[:outs], acc[outs:]
        rows = slice(u * outs, (u + 1) * outs)
        for q in many:
            cut = slice((q - first) * LANES, (q - first + 1) * LANES)
            filt[q, 0, rows] = real[:, cut]
            filt[q, 1, rows] = imag[:, cut]
        power[rows, (first + 1) * LANES : (first + cuts + 1) * LANES] = (
            real * real + imag * imag
        ).astype(bf16)


def whiten_cut(q, band, pick, filt, power, own, mine):
    rounds = own.shape[0] // filt.shape[0]
    chans = own.shape[2]
    smooth = jnp.dot(
        power[:, q * LANES : (q + 3) * LANES], band[...], preferred_element_type=f32
    )
    scale = lax.rsqrt(smooth * (1.0 / SMOOTH) + water_level)
    for p in range(2):
        white = (filt[q, p] * scale).astype(bf16)
        res = jnp.dot(pick[...], white, preferred_element_type=f32).astype(bf16)
        for r in range(rounds):
            own[q * rounds + r, p] = res[r * chans : (r + 1) * chans]
        at = rounds * chans
        for b in range(mine.shape[1]):
            mine[q, b, p] = res[at + b * chans : at + (b + 1) * chans]


def row_kernel(
    rows,
    owner_in,
    own_in,
    bank_in,
    index_in,
    mask_in,
    offset_in,
    loc_ref,
    src_ref,
    part_ref,
    owner_ref,
    own_ref,
    bank_ref,
    index_ref,
    mask_ref,
    offset_ref,
    in_sems,
    raw,
    masks,
    toep,
    band,
    pick,
    filt,
    power,
    mine,
    back,
    line_buf,
    done,
    across,
    beside,
    raw_send,
    raw_recv,
    mask_sems,
    back_sems,
    line_sems,
    give_sems,
    give_recv,
):
    wins, chans = mask_ref.shape
    cuts = raw.shape[0]
    nbank = bank_ref.shape[1]
    parts = wins
    rounds = owner_ref.shape[0]
    me = lax.axis_index("chan")
    core = me % 2
    place = me % parts
    base = me - place
    row = me // parts
    partner = me + 1 - 2 * core
    alike = base + (place + 2) % parts
    partner_place = place + 1 - 2 * core
    alike_place = (place + 2) % parts
    corner_place = (partner_place + 2) % parts
    mesh_id = pl.DeviceIdType.MESH

    def send(src, dst, send_sem, recv_sem, who):
        return pltpu.make_async_remote_copy(
            src_ref=src,
            dst_ref=dst,
            send_sem=send_sem,
            recv_sem=recv_sem,
            device_id={"chan": who},
            device_id_type=mesh_id,
        )

    pairs_in = [
        (own_in, own_ref),
        (mask_in, mask_ref),
        (bank_in, bank_ref),
        (index_in, index_ref),
        (offset_in, offset_ref),
        (owner_in, owner_ref),
    ]
    inputs = [
        pltpu.make_async_copy(src, dst, in_sems.at[n]) for n, (src, dst) in enumerate(pairs_in)
    ]
    for copy in inputs:
        copy.start()

    barrier = pltpu.get_barrier_semaphore()
    partners = [(place != j, base + j) for j in range(parts)]
    for j in range(parts):
        near = jnp.logical_or(place == j, jnp.logical_or(place == parts - 1, j == 0))
        partners.append((jnp.logical_and(row < rows - 1, near), base + parts + j))
        near = jnp.logical_or(place == j, jnp.logical_or(place == 0, j == parts - 1))
        partners.append((jnp.logical_and(row > 0, near), base - parts + j))
    expected = jnp.int32(0)
    for there, who in partners:
        expected += there.astype(jnp.int32)

        @pl.when(there)
        def _(who=who):
            pl.semaphore_signal(barrier, inc=1, device_id={"chan": who}, device_id_type=mesh_id)

    pl.semaphore_wait(barrier, expected)

    peers = [alike_place, corner_place, partner_place]

    def raw_copy(q, to, slot, n, who):
        return send(
            own_ref.at[:, to, :, q * LANES : (q + 1) * LANES],
            raw.at[q, slot],
            raw_send.at[min(n // (parts - 1), 1)],
            raw_recv.at[q],
            who,
        )

    def mask_copy(n):
        return send(
            mask_ref, masks.at[place], mask_sems.at[0], mask_sems.at[1], base + peers[n]
        )

    above = jnp.logical_and(place == parts - 1, row < rows - 1)
    below = jnp.logical_and(place == 0, row > 0)

    def edges(q, act):
        @pl.when(above)
        def _():
            for j in range(parts):
                act(raw_copy(q, j, 0, parts - 1 + j, base + parts + j))

        @pl.when(below)
        def _():
            for j in range(parts):
                act(raw_copy(q, j, parts + 1, parts - 1 + j, base - parts + j))

    for copy in inputs:
        copy.wait()
    for n in range(parts - 1):
        mask_copy(n).start()
    for q in range(cuts):
        for n in range(2):
            raw_copy(q, peers[n], 1 + place, n, base + peers[n]).start()
        edges(q, lambda copy: copy.start())
        raw_copy(q, peers[2], 1 + place, 2, base + peers[2]).start()

    masks[place] = mask_ref[...]
    for q in range(cuts):
        raw[q, 1 + place] = own_ref[:, place, :, q * LANES : (q + 1) * LANES]

    @pl.when(row == 0)
    def _():
        raw[:, 0] = jnp.zeros_like(raw[:, 0])

    @pl.when(row == rows - 1)
    def _():
        raw[:, parts + 1] = jnp.zeros_like(raw[:, parts + 1])

    line = Chain(row, rows, lambda i: i * parts + place, HOP, (*line_buf, line_sems))
    line.clear()
    build_bank(bank_ref, toep)
    build_band(band)
    edge = jnp.zeros((power.shape[0], LANES), bf16)
    power[:, :LANES] = edge
    power[:, (cuts + 1) * LANES :] = edge

    def whole(ref, send_sem, recv_sem):
        return send(ref, ref, send_sem, recv_sem, partner)

    whole(masks.at[: parts - 1], mask_sems.at[0], mask_sems.at[1]).wait_recv()
    build_pick(base, place, owner_ref, offset_ref, masks, pick)

    some = back.at[:, : parts - 1]
    count = line.count
    last = HOP * (rows - 1)

    def give(src, dst, n, k, who):
        return send(src.at[k], dst, give_sems.at[n], give_recv.at[(n + 1) // 2, k], who)

    def put(k, j, value):
        src_ref[k, j] = value.astype(f32) * (1.0 / wins)

    def tick(t):
        line.tick(t)
        k = t - last

        @pl.when(jnp.logical_and(k >= 0, k < count))
        def _():
            total = line.result(k)
            done[k] = total
            give(done, across.at[k], 0, k, alike).start()
            give(done, beside.at[k, 0], 1, k, partner).start()
            put(k, place, total)

        q = t - last - SIDE

        @pl.when(jnp.logical_and(q >= 0, q < count))
        def _():
            give(done, across.at[q], 0, q, alike).wait_recv()
            give(across, beside.at[q, 1], 2, q, partner).start()
            put(q, alike_place, across[q])

        b = t - last - SIDE - NEAR

        @pl.when(jnp.logical_and(b >= 0, b < count))
        def _():
            whole(beside.at[b], give_sems.at[1], give_recv.at[1, b]).wait_recv()
            put(b, partner_place, beside[b, 0])
            put(b, corner_place, beside[b, 1])

        @pl.when(b == 0)
        def _():
            whole(some, back_sems.at[0], back_sems.at[1]).wait_recv()
            loc_ref[...] = back[...]

        r = b % rounds

        @pl.when(jnp.logical_and(jnp.logical_and(b >= 0, b < count), r < rounds - 1))
        def _():
            at = b // rounds
            cut = pl.ds(pl.multiple_of(at * LANES, LANES), LANES)
            loc = [[back[at, w, p] for w in range(wins)] for p in range(2)]

            def wide(w, p, j):
                return src_ref[b, w, p, pl.ds(j, 1), :]

            def keep(j, real, imag):
                part_ref[0, r * chans + j, :, cut] = real
                part_ref[1, r * chans + j, :, cut] = imag

            products(wide, loc, keep, chans)

    def back_copy(q, n):
        return send(
            mine.at[q, peers[n]],
            back.at[q, place],
            back_sems.at[0],
            back_sems.at[1],
            base + peers[n],
        )

    def pass_on(q):
        back[q, place] = mine[q, place]

        @pl.loop(q * rounds, (q + 1) * rounds)
        def _(t):
            if last < count:
                tick(t)
            else:
                line.tick(t)

        for n in range(parts - 1):
            back_copy(q, n).start()

    def finish(q):
        whiten_cut(q, band, pick, filt, power, line.own, mine)
        pass_on(q)

    inner = jnp.logical_and(row > 0, row < rows - 1)
    outer = jnp.logical_or(row == 0, row == rows - 1)
    half = cuts // 2
    for first in (0, half):
        for q in range(first, first + half):
            for there, many in ((inner, parts + 1), (outer, parts)):

                @pl.when(there)
                def _(q=q, many=many):
                    whole(raw.at[q, :many], raw_send.at[0], raw_recv.at[q]).wait_recv()

        filter_cuts(first, half, nbank, raw, toep, index_ref, filt, power)
        if first == 0:
            for q in range(half - 1):
                finish(q)
    for q in range(half - 1, cuts):
        whiten_cut(q, band, pick, filt, power, line.own, mine)
    for q in range(half - 1, cuts):
        pass_on(q)

    @pl.loop(cuts * rounds, count + last + SIDE + NEAR)
    def _(t):
        tick(t)

    whole(some, back_sems.at[0], back_sems.at[1]).wait_send()
    whole(masks.at[: parts - 1], mask_sems.at[0], mask_sems.at[1]).wait_send()
    whole(raw.at[:, : parts - 1], raw_send.at[0], raw_recv.at[0]).wait_send()

    @pl.when(jnp.logical_or(above, below))
    def _():
        whole(raw.at[:, :parts], raw_send.at[1], raw_recv.at[0]).wait_send()

    line.drain(partner)
    for n in range(3):
        whole(done, give_sems.at[n], give_recv.at[0, 0]).wait_send()


def row_front(rows, owner, own, bank, index, mask, offset):
    _, wins, chans, bins = own.shape
    nbank = bank.shape[1]
    rounds = owner.shape[0]
    cuts = bins // LANES
    parts = wins
    count = cuts * rounds
    outs = LANES // 2
    vmem = pl.BlockSpec(memory_space=pltpu.VMEM)
    chunk = (2, chans, LANES)
    chunks = pltpu.VMEM((count, *chunk), bf16)
    return pl.pallas_call(
        functools.partial(row_kernel, rows),
        out_shape=[
            pltpu.VMEM((cuts, wins, *chunk), bf16),
            pltpu.VMEM((count, wins, *chunk), f32),
            pltpu.VMEM((2, (rounds - 1) * chans, chans, bins), bf16),
        ],
        in_specs=[pl.BlockSpec(memory_space=pltpu.HBM)] * 6,
        out_specs=[vmem] * 3,
        scratch_shapes=[
            pltpu.SMEM(owner.shape, owner.dtype),
            *[pltpu.VMEM(a.shape, a.dtype) for a in (own, bank, index, mask, offset)],
            pltpu.SemaphoreType.DMA((6,)),
            pltpu.VMEM((cuts, parts + 2, *chunk), bf16),
            pltpu.VMEM((parts, wins, chans), jnp.int32),
            pltpu.VMEM((nbank * 2 * outs, 4 * LANES), bf16),
            pltpu.VMEM((3 * LANES, LANES), bf16),
            pltpu.VMEM(((rounds + parts) * chans, parts * chans), bf16),
            pltpu.VMEM((cuts, 2, parts * chans, LANES), f32),
            pltpu.VMEM((parts * chans, (cuts + 2) * LANES), bf16),
            pltpu.VMEM((cuts, parts, *chunk), bf16),
            pltpu.VMEM((cuts, parts, *chunk), bf16),
            [chunks] * 5,
            chunks,
            chunks,
            pltpu.VMEM((count, 2, *chunk), bf16),
            pltpu.SemaphoreType.DMA((2,)),
            pltpu.SemaphoreType.DMA((cuts,)),
            pltpu.SemaphoreType.DMA((2,)),
            pltpu.SemaphoreType.DMA((2,)),
            pltpu.SemaphoreType.DMA((2, count + 1)),
            pltpu.SemaphoreType.DMA((3,)),
            pltpu.SemaphoreType.DMA((2, count)),
        ],
        compiler_params=pltpu.CompilerParams(
            collective_id=0, has_side_effects=True, vmem_limit_bytes=24 << 20
        ),
        name="front",
    )(*[pltpu.with_memory_space_constraint(a, pltpu.HBM) for a in (owner, own, bank, index, mask, offset)])


def products(wide, loc, put, count):
    wins = len(loc[0])
    chans = loc[0][0].shape[0]

    def one(j, carry):
        src = [
            [
                jnp.broadcast_to(wide(w, p, j), (chans, LANES)).astype(bf16)
                for w in range(wins)
            ]
            for p in range(2)
        ]
        real = tree_sum([src[p][w] * loc[p][w] for w in range(wins) for p in range(2)])
        plus = tree_sum([src[0][w] * loc[1][w] for w in range(wins)])
        minus = tree_sum([src[1][w] * loc[0][w] for w in range(wins)])
        put(j, real, plus - minus)
        return carry

    lax.fori_loop(0, count, one, 0, unroll=8)


def pairs_kernel(src_ref, loc_ref, part_ref, out_ref, buf, sems):
    cuts, wins, _, chans, _ = loc_ref.shape
    steps, _, per = buf.shape[:3]
    rounds = src_ref.shape[0] // cuts
    ready = rounds - 1

    def flush(r):
        rows = slice(r * chans, (r + 1) * chans)
        return pltpu.make_async_copy(part_ref.at[:, rows], out_ref.at[:, rows], sems.at[r])

    def last(step):
        at = ready * chans + step * per
        return pltpu.make_async_copy(
            buf.at[step], out_ref.at[:, at : at + per], sems.at[ready + step]
        )

    for r in range(ready):
        flush(r).start()
    for step in range(steps):
        for q in range(cuts):
            loc = [[loc_ref[q, w, p] for w in range(wins)] for p in range(2)]

            def wide(w, p, j, q=q, step=step):
                return src_ref[q * rounds + ready, w, p, pl.ds(step * per + j, 1), :]

            def put(j, real, imag, q=q, step=step):
                cut = slice(q * LANES, (q + 1) * LANES)
                buf[step, 0, j, :, cut] = real
                buf[step, 1, j, :, cut] = imag

            products(wide, loc, put, per)
        last(step).start()
    for r in range(ready):
        flush(r).wait()
    for step in range(steps):
        last(step).wait()


def pairs(src, loc, part):
    cuts, wins, _, chans, _ = loc.shape
    rounds = src.shape[0] // cuts
    steps = 2
    vmem = pl.BlockSpec(memory_space=pltpu.VMEM)
    return pl.pallas_call(
        pairs_kernel,
        out_shape=jax.ShapeDtypeStruct((2, rounds * chans, chans, cuts * LANES), bf16),
        in_specs=[vmem] * 3,
        out_specs=pl.BlockSpec(memory_space=pl.ANY),
        scratch_shapes=[
            pltpu.VMEM((steps, 2, chans // steps, chans, cuts * LANES), bf16),
            pltpu.SemaphoreType.DMA((rounds - 1 + steps,)),
        ],
        compiler_params=pltpu.CompilerParams(vmem_limit_bytes=16 << 20),
        name="pairs",
    )(src, loc, part)


def body(spectra, filter_bank, band_index, window_mask, owner_order, source_offset):
    grid = chip_grid(lax.axis_size("chan"))
    _, wins, chans, bins = spectra.shape
    ntap = filter_bank.shape[2]
    if 2 * grid[1] == wins == 4 and 4 * chans == LANES and ntap == 2 * chans + 1:
        whitened, sources, part = row_front(
            grid[0],
            owner_order,
            spectra,
            filter_bank,
            band_index[None, :],
            window_mask,
            source_offset,
        )
        return pairs(sources, whitened, part)
    whitened, sources = front(
        grid, owner_order, spectra, filter_bank, band_index[None, :], window_mask
    )
    sources = sources.reshape(sources.shape[0], wins, 2, chans, bins)
    return cross(source_offset, sources, whitened)


def solution(mesh):
    in_specs = (
        P(None, "groups", "chan", None),
        P(),
        P(),
        P("groups", "chan"),
        P("groups"),
        P("groups", None),
    )
    out_specs = P(None, "groups", "chan", None)
    return jax.shard_map(body, mesh=mesh, in_specs=in_specs, out_specs=out_specs, check_vma=False)
```

```python
import functools

import jax
import jax.numpy as jnp
from jax import lax
from jax.experimental import pallas as pl
from jax.experimental.pallas import tpu as pltpu
from jax.sharding import PartitionSpec as P

SMOOTH = 17
water_level = 0.05
bf16 = jnp.bfloat16
f32 = jnp.float32
LANES = 128
LAG = 4


def split(x):
    hi = x.astype(bf16)
    return hi, (x - hi.astype(f32)).astype(bf16)


def build_toeplitz(bank_ref, toep):
    _, nbank, ntap = bank_ref.shape
    chans = toep.shape[1] // (2 * nbank)
    for b in range(nbank):
        parts = []
        for p in range(2):
            row = jnp.concatenate(
                [bank_ref[p, b : b + 1, :], jnp.zeros((1, LANES - ntap), f32)], axis=1
            )
            full = jnp.broadcast_to(row, (chans, LANES))
            parts.append(split(pltpu.roll(full, 0, 1, stride=1, stride_axis=0)))
        at = b * 2 * chans
        for part in range(2):
            real, imag = parts[0][part], parts[1][part]
            toep[part, at : at + chans, :LANES] = real
            toep[part, at : at + chans, LANES:] = -imag
            toep[part, at + chans : at + 2 * chans, :LANES] = imag
            toep[part, at + chans : at + 2 * chans, LANES:] = real


def build_window(band):
    bins = band.shape[0]
    rows = lax.broadcasted_iota(jnp.int32, (bins, bins), 0)
    cols = lax.broadcasted_iota(jnp.int32, (bins, bins), 1)
    band[...] = (jnp.abs(rows - cols) <= SMOOTH // 2).astype(f32).astype(bf16)


def filter_window(nbank, w, x, toep, index_ref, filt, power):
    bins = filt.shape[2]
    chans = toep.shape[1] // (2 * nbank)
    tile = 256
    rows = slice(w * chans, (w + 1) * chans)
    for n in range(bins // tile):
        cut = slice(n * tile, (n + 1) * tile)
        here = x(cut)
        res = jnp.dot(toep[0], here, preferred_element_type=f32)
        res += jnp.dot(toep[1], here, preferred_element_type=f32)
        index = index_ref[:, cut]
        acc = res[: 2 * chans]
        for b in range(1, nbank):
            acc = jnp.where(index == b, res[2 * chans * b : 2 * chans * (b + 1)], acc)
        real, imag = acc[:chans], acc[chans:]
        filt[0, rows, cut] = real
        filt[1, rows, cut] = imag
        hi, lo = split(real * real + imag * imag)
        power[0, rows, cut] = hi
        power[1, rows, cut] = lo


def whiten_window(w, band, mask_ref, filt, power):
    chans = mask_ref.shape[1]
    rows = slice(w * chans, (w + 1) * chans)
    smooth = jnp.dot(power[0, rows], band[...], preferred_element_type=f32)
    smooth += jnp.dot(power[1, rows], band[...], preferred_element_type=f32)
    scale = lax.rsqrt(smooth * (1.0 / SMOOTH) + water_level)
    eye = lax.broadcasted_iota(jnp.int32, (chans, chans), 0) == lax.broadcasted_iota(
        jnp.int32, (chans, chans), 1
    )
    row = jnp.broadcast_to(mask_ref[w : w + 1, :].astype(f32), (chans, chans))
    valid = jnp.sum(jnp.where(eye, row, 0.0), axis=1, keepdims=True)
    scale = scale * valid
    return [(filt[p, rows] * scale).astype(bf16) for p in range(2)]


class Line:
    def __init__(self, pos, length, device_of, lag, refs):
        self.pos, self.length, self.device_of, self.lag = pos, length, device_of, lag
        self.own, self.out_r, self.out_l, self.in_r, self.in_l, self.sems = refs
        self.count = self.own.shape[0]

    def clear(self):
        @pl.when(self.pos == 0)
        def _():
            self.in_r[...] = jnp.zeros_like(self.in_r)

        @pl.when(self.pos == self.length - 1)
        def _():
            self.in_l[...] = jnp.zeros_like(self.in_l)

    def copy(self, way, k):
        out, into = (self.out_r, self.in_r) if way == 0 else (self.out_l, self.in_l)
        other = self.pos + 1 if way == 0 else self.pos - 1
        return pltpu.make_async_remote_copy(
            src_ref=out.at[k],
            dst_ref=into.at[k],
            send_sem=self.sems.at[way, 0, k],
            recv_sem=self.sems.at[way, 1, k],
            device_id={"chan": self.device_of(other)},
            device_id_type=pl.DeviceIdType.MESH,
        )

    def tick(self, t):
        for way in range(2):
            behind = self.pos if way == 0 else self.length - 1 - self.pos
            out, into = (self.out_r, self.in_r) if way == 0 else (self.out_l, self.in_l)
            k = t - self.lag * behind
            inside = jnp.logical_and(k >= 0, k < self.count)

            @pl.when(jnp.logical_and(inside, behind > 0))
            def _(way=way, k=k):
                self.copy(way, k).wait_recv()

            @pl.when(jnp.logical_and(inside, behind < self.length - 1))
            def _(way=way, k=k, out=out, into=into):
                out[k] = self.own[k] + into[k]
                self.copy(way, k).start()

    def result(self, k):
        return self.own[k] + self.in_r[k] + self.in_l[k]

    def drain(self):
        for way in range(2):
            behind = self.pos if way == 0 else self.length - 1 - self.pos

            @pl.when(behind < self.length - 1)
            def _(way=way):
                @pl.loop(0, self.count)
                def _(k):
                    self.copy(way, k).wait_send()


def front_kernel(
    rows,
    cols,
    owner_ref,
    own_ref,
    bank_ref,
    index_ref,
    mask_ref,
    out_ref,
    src_ref,
    halo,
    toep,
    band,
    filt,
    power,
    mine,
    beside,
    row_buf,
    done,
    gathered,
    halo_sems,
    beside_sems,
    row_sems,
    gather_sems,
):
    wins, chans = mask_ref.shape
    bins = own_ref.shape[3]
    parts = 2 * cols
    subs, piece = beside.shape[1], beside.shape[2]
    me = lax.axis_index("chan")
    size = rows * cols * 2
    core = me % 2
    place = me % (2 * cols)
    base = me - place
    row = me // (2 * cols)
    partner = me + 1 - 2 * core
    mesh_id = pl.DeviceIdType.MESH

    barrier = pltpu.get_barrier_semaphore()
    partners = [
        (me > 0, me - 1),
        (me < size - 1, me + 1),
        (row > 0, me - 2 * cols),
        (row < rows - 1, me + 2 * cols),
    ] + [(place != j, base + j) for j in range(2 * cols)]
    expected = jnp.int32(0)
    for there, who in partners:
        expected += there.astype(jnp.int32)

        @pl.when(there)
        def _(who=who):
            pl.semaphore_signal(barrier, inc=1, device_id={"chan": who}, device_id_type=mesh_id)

    pl.semaphore_wait(barrier, expected)

    def halo_copy(way, w):
        return pltpu.make_async_remote_copy(
            src_ref=own_ref.at[:, w],
            dst_ref=halo.at[way, :, w],
            send_sem=halo_sems.at[way, 0, w],
            recv_sem=halo_sems.at[way, 1, w],
            device_id={"chan": me + 1 - 2 * way},
            device_id_type=mesh_id,
        )

    order = list(range(wins))
    sends = (me < size - 1, me > 0)
    for w in order:
        for way in range(2):

            @pl.when(sends[way])
            def _(way=way, w=w):
                halo_copy(way, w).start()

    for way in range(2):

        @pl.when(jnp.logical_not(sends[1 - way]))
        def _(way=way):
            halo[way] = jnp.zeros_like(halo[way])

    line = Line(row, rows, lambda i: i * 2 * cols + place, LAG, (*row_buf, row_sems))
    line.clear()
    build_toeplitz(bank_ref, toep)
    build_window(band)

    def beside_copy(sender, j):
        return pltpu.make_async_remote_copy(
            src_ref=mine.at[pl.ds(j * subs, subs)],
            dst_ref=beside.at[sender],
            send_sem=beside_sems.at[0, j],
            recv_sem=beside_sems.at[1, sender],
            device_id={"chan": base + j},
            device_id_type=mesh_id,
        )

    blank = jnp.zeros((LANES - 3 * chans, bins), bf16)
    for w in order:
        for way in range(2):

            @pl.when(sends[1 - way])
            def _(way=way, w=w):
                halo_copy(way, w).wait_recv()

        def x(cut, w=w):
            stack = []
            for p in range(2):
                stack += [halo[0, p, w, :, cut], own_ref[p, w, :, cut], halo[1, p, w, :, cut]]
                stack += [blank[:, cut]]
            return jnp.concatenate(stack, axis=0)

        filter_window(bank_ref.shape[1], w, x, toep, index_ref, filt, power)
        white = whiten_window(w, band, mask_ref, filt, power)
        for p in range(2):
            out_ref[p, w] = white[p]
            for i in range(chans // piece):
                mine[(w * 2 + p) * (chans // piece) + i] = white[p][i * piece : (i + 1) * piece]
        for j in range(w * parts // wins, (w + 1) * parts // wins):

            @pl.when(place != j)
            def _(j=j):
                beside_copy(place, j).start()

    beside[place] = mine[pl.ds(place * subs, subs)]
    for j in range(parts):

        @pl.when(place != j)
        def _(j=j):
            beside_copy(j, j).wait_recv()

    count = line.count

    @pl.loop(0, count)
    def _(k):
        total = jnp.zeros((piece, bins), bf16)
        for j in range(parts):
            total += beside[j, k % subs] * (owner_ref[k // subs] == base + j).astype(f32).astype(bf16)
        line.own[k] = total

    def give(src, origin, k, sem, who):
        return pltpu.make_async_remote_copy(
            src_ref=src,
            dst_ref=gathered.at[origin, k],
            send_sem=gather_sems.at[sem, k],
            recv_sem=gather_sems.at[2 * parts + origin, k],
            device_id={"chan": who},
            device_id_type=mesh_id,
        )

    def put(j, k, value):
        src_ref[k // subs, j * subs + k % subs] = value

    alike = [jnp.logical_and(place != j, core == j % 2) for j in range(parts)]
    last = LAG * (rows - 1)

    @pl.loop(0, count + last + LAG)
    def _(t):
        line.tick(t)
        k = t - last

        @pl.when(jnp.logical_and(k >= 0, k < count))
        def _():
            total = line.result(k)
            done[k] = total
            for j in range(parts):

                @pl.when(alike[j])
                def _(j=j):
                    give(done.at[k], place, k, j, base + j).start()

            give(done.at[k], place, k, parts + place, partner).start()
            put(place, k, total)

        q = t - last - LAG

        @pl.when(q >= 0)
        def _():
            for j in range(parts):

                @pl.when(alike[j])
                def _(j=j):
                    give(done.at[q], j, q, j, partner).wait_recv()
                    give(gathered.at[j, q], j, q, parts + j, partner).start()
                    put(j, q, gathered[j, q])

    @pl.loop(0, count)
    def _(k):
        for j in range(parts):

            @pl.when(core != j % 2)
            def _(j=j):
                give(done.at[k], j, k, j, partner).wait_recv()
                put(j, k, gathered[j, k])

    for way in range(2):
        for w in range(wins):

            @pl.when(sends[way])
            def _(way=way, w=w):
                halo_copy(way, w).wait_send()

    for j in range(parts):

        @pl.when(place != j)
        def _(j=j):
            beside_copy(place, j).wait_send()

    line.drain()

    @pl.loop(0, count)
    def _(k):
        give(done.at[k], place, k, parts + place, partner).wait_send()
        for j in range(parts):

            @pl.when(alike[j])
            def _(j=j):
                give(done.at[k], place, k, j, partner).wait_send()
                give(gathered.at[j, k], j, k, parts + j, partner).wait_send()


def front(grid, owner, own, bank, index, mask):
    _, wins, chans, bins = own.shape
    nbank = bank.shape[1]
    rounds = owner.shape[0]
    rows, cols = grid
    parts = 2 * cols
    total = wins * 2 * chans
    piece = min(chans, total // parts)
    subs = total // parts // piece
    count = rounds * subs
    vmem = pl.BlockSpec(memory_space=pltpu.VMEM)
    chunk = (piece, bins)
    chunks = pltpu.VMEM((count, *chunk), bf16)
    return pl.pallas_call(
        functools.partial(front_kernel, rows, cols),
        out_shape=[
            jax.ShapeDtypeStruct(own.shape, bf16),
            jax.ShapeDtypeStruct((rounds, parts * subs, piece, bins), bf16),
        ],
        in_specs=[pl.BlockSpec(memory_space=pltpu.SMEM)] + [vmem] * 4,
        out_specs=[vmem] * 2,
        scratch_shapes=[
            pltpu.VMEM((2, *own.shape), bf16),
            pltpu.VMEM((2, nbank * 2 * chans, 2 * LANES), bf16),
            pltpu.VMEM((bins, bins), bf16),
            pltpu.VMEM((2, wins * chans, bins), f32),
            pltpu.VMEM((2, wins * chans, bins), bf16),
            pltpu.VMEM((parts * subs, *chunk), bf16),
            pltpu.VMEM((parts, subs, *chunk), bf16),
            [chunks] * 5,
            chunks,
            pltpu.VMEM((parts, count, *chunk), bf16),
            pltpu.SemaphoreType.DMA((2, 2, wins)),
            pltpu.SemaphoreType.DMA((2, parts)),
            pltpu.SemaphoreType.DMA((2, 2, count)),
            pltpu.SemaphoreType.DMA((3 * parts, count)),
        ],
        compiler_params=pltpu.CompilerParams(collective_id=0, has_side_effects=True),
        name="front",
    )(owner, own, bank, index, mask)


def tree_sum(terms):
    while len(terms) > 1:
        terms = [a + b for a, b in zip(terms[::2], terms[1::2])]
    return terms[0]


def cross_kernel(offset_ref, src_ref, loc_ref, out_ref, wide, held):
    _, wins, chans, bins = loc_ref.shape
    count = out_ref.shape[1]
    r, h = pl.program_id(0), pl.program_id(1)

    @pl.when(jnp.logical_and(r == 0, h == 0))
    def _():
        held[...] = loc_ref[...]

    @pl.when(h == 0)
    def _():
        for p in range(2):
            for w in range(wins):
                wide[:, p * wins + w, :] = src_ref[0, w, p].astype(f32) * (1.0 / wins)

    for n in range(bins // LANES):
        cut = slice(n * LANES, (n + 1) * LANES)

        def one(j, carry, cut=cut):
            loc = [[held[p, w, :, cut] for w in range(wins)] for p in range(2)]
            at = offset_ref[r, h * count + j]
            src = [
                [
                    jnp.broadcast_to(
                        wide[at, p * wins + w : p * wins + w + 1, cut], (chans, LANES)
                    ).astype(bf16)
                    for w in range(wins)
                ]
                for p in range(2)
            ]
            real = tree_sum(
                [src[p][w] * loc[p][w] for w in range(wins) for p in range(2)]
            )
            plus = tree_sum([src[0][w] * loc[1][w] for w in range(wins)])
            minus = tree_sum([src[1][w] * loc[0][w] for w in range(wins)])
            out_ref[0, j, :, cut] = real
            out_ref[1, j, :, cut] = plus - minus
            return carry

        lax.fori_loop(0, count, one, 0, unroll=4)


def cross(offset, src, loc, blocks=1):
    rounds, wins, _, chans, bins = src.shape
    per = chans // blocks
    return pl.pallas_call(
        cross_kernel,
        out_shape=jax.ShapeDtypeStruct((2, rounds * chans, chans, bins), bf16),
        grid=(rounds, blocks),
        in_specs=[
            pl.BlockSpec(memory_space=pltpu.SMEM),
            pl.BlockSpec((1, wins, 2, chans, bins), lambda r, h: (r, 0, 0, 0, 0)),
            pl.BlockSpec((2, wins, chans, bins), lambda r, h: (0, 0, 0, 0)),
        ],
        out_specs=pl.BlockSpec((2, per, chans, bins), lambda r, h: (0, r * blocks + h, 0, 0)),
        scratch_shapes=[
            pltpu.VMEM((chans, 2 * wins, bins), f32),
            pltpu.VMEM((2, wins, chans, bins), bf16),
        ],
        name="cross",
    )(offset, src, loc)


def chip_grid(size):
    chips = size // 2
    cols = 1
    while cols * cols * 4 <= chips:
        cols *= 2
    return chips // cols, cols


HOP, SIDE, NEAR, LATE = 10, 8, 4, 7


class Chain(Line):
    def copy(self, way, k):
        out, into = (self.out_r, self.in_r) if way == 0 else (self.out_l, self.in_l)
        other = self.pos + 1 if way == 0 else self.pos - 1
        return self.make(way, out.at[k], into.at[k], k, self.device_of(other))

    def make(self, way, src, dst, k, who):
        return pltpu.make_async_remote_copy(
            src_ref=src,
            dst_ref=dst,
            send_sem=self.sems.at[way, self.count],
            recv_sem=self.sems.at[way, k],
            device_id={"chan": who},
            device_id_type=pl.DeviceIdType.MESH,
        )

    def drain(self, who):
        for way in range(2):
            behind = self.pos if way == 0 else self.length - 1 - self.pos
            out = self.out_r if way == 0 else self.out_l

            @pl.when(behind < self.length - 1)
            def _(way=way, out=out):
                self.make(way, out, out, 0, who).wait_send()


def build_bank(bank_ref, toep):
    _, nbank, ntap = bank_ref.shape
    outs = toep.shape[0] // (2 * nbank)
    for b in range(nbank):
        parts = []
        for p in range(2):
            row = jnp.concatenate(
                [bank_ref[p, b : b + 1, :], jnp.zeros((1, LANES - ntap), f32)], axis=1
            )
            full = jnp.broadcast_to(row, (outs, LANES))
            parts.append(split(pltpu.roll(full, 0, 1, stride=1, stride_axis=0)))
        at = b * 2 * outs
        for part in range(2):
            real, imag = parts[0][part], parts[1][part]
            left = slice(2 * part * LANES, (2 * part + 1) * LANES)
            right = slice((2 * part + 1) * LANES, (2 * part + 2) * LANES)
            toep[at : at + outs, left] = real
            toep[at : at + outs, right] = -imag
            toep[at + outs : at + 2 * outs, left] = imag
            toep[at + outs : at + 2 * outs, right] = real


def build_band(band):
    wide, bins = band.shape
    rows = lax.broadcasted_iota(jnp.int32, (wide, bins), 0)
    cols = lax.broadcasted_iota(jnp.int32, (wide, bins), 1)
    band[...] = (jnp.abs(rows - bins - cols) <= SMOOTH // 2).astype(f32).astype(bf16)


def build_pick(base, place, owner_ref, offset_ref, masks, pick):
    parts, _, chans = masks.shape
    rounds = offset_ref.shape[0]
    total = parts * chans
    valid = jnp.concatenate(
        [masks[b, pl.ds(place, 1), :].astype(f32) for b in range(parts)], axis=1
    )
    eye = lax.broadcasted_iota(jnp.int32, (chans, chans), 0) == lax.broadcasted_iota(
        jnp.int32, (chans, chans), 1
    )
    cols = lax.broadcasted_iota(jnp.int32, (chans, total), 1).astype(f32)
    for r in range(rounds):
        row = jnp.broadcast_to(offset_ref[r : r + 1, :].astype(f32), (chans, chans))
        col = jnp.sum(jnp.where(eye, row, 0.0), axis=1, keepdims=True)
        col = col + ((owner_ref[r] - base) * chans).astype(f32)
        pick[r * chans : (r + 1) * chans] = jnp.where(cols == col, valid, 0.0).astype(bf16)
    rows = lax.broadcasted_iota(jnp.int32, (total, total), 0)
    same = rows == lax.broadcasted_iota(jnp.int32, (total, total), 1)
    pick[rounds * chans :] = jnp.where(same, valid, 0.0).astype(bf16)


def filter_cuts(first, cuts, nbank, raw, toep, index_ref, filt, power):
    outs = toep.shape[0] // (2 * nbank)
    blocks, chans = raw.shape[1], raw.shape[3]
    step = outs // chans
    many = range(first, first + cuts)
    index = index_ref[:, first * LANES : (first + cuts) * LANES]
    for u in range((blocks - 2) // step):
        here = [
            raw[first // cuts, u * step : u * step + step + 2, p].reshape(
                (step + 2) * chans, cuts * LANES
            )
            for p in range(2)
        ]
        res = jnp.dot(
            toep[...], jnp.concatenate(here + here, axis=0), preferred_element_type=f32
        )
        acc = res[: 2 * outs]
        for b in range(1, nbank):
            acc = jnp.where(index == b, res[2 * outs * b : 2 * outs * (b + 1)], acc)
        real, imag = acc[:outs], acc[outs:]
        rows = slice(u * outs, (u + 1) * outs)
        for q in many:
            cut = slice((q - first) * LANES, (q - first + 1) * LANES)
            filt[q, 0, rows] = real[:, cut]
            filt[q, 1, rows] = imag[:, cut]
        power[rows, (first + 1) * LANES : (first + cuts + 1) * LANES] = (
            real * real + imag * imag
        ).astype(bf16)


def whiten_cut(q, band, pick, filt, power, own, mine):
    rounds = own.shape[0] // filt.shape[0]
    chans = own.shape[2]
    smooth = jnp.dot(
        power[:, q * LANES : (q + 3) * LANES], band[...], preferred_element_type=f32
    )
    scale = lax.rsqrt(smooth * (1.0 / SMOOTH) + water_level)
    for p in range(2):
        white = (filt[q, p] * scale).astype(bf16)
        res = jnp.dot(pick[...], white, preferred_element_type=f32).astype(bf16)
        for r in range(rounds):
            own[q * rounds + r, p] = res[r * chans : (r + 1) * chans]
        at = rounds * chans
        for b in range(mine.shape[1]):
            mine[q, b, p] = res[at + b * chans : at + (b + 1) * chans]


def row_kernel(
    rows,
    owner_in,
    own_in,
    bank_in,
    index_in,
    mask_in,
    offset_in,
    loc_ref,
    src_ref,
    part_ref,
    owner_ref,
    own_ref,
    bank_ref,
    index_ref,
    mask_ref,
    offset_ref,
    in_sems,
    raw,
    masks,
    toep,
    band,
    pick,
    filt,
    power,
    mine,
    back,
    line_buf,
    done,
    across,
    beside,
    raw_send,
    raw_recv,
    mask_sems,
    back_sems,
    line_sems,
    give_sems,
    give_recv,
):
    wins, chans = mask_ref.shape
    halves, span = raw.shape[0], raw.shape[4]
    cuts = halves * span // LANES
    nbank = bank_ref.shape[1]
    parts = wins
    rounds = owner_ref.shape[0]
    me = lax.axis_index("chan")
    core = me % 2
    place = me % parts
    base = me - place
    row = me // parts
    partner = me + 1 - 2 * core
    alike = base + (place + 2) % parts
    partner_place = place + 1 - 2 * core
    alike_place = (place + 2) % parts
    corner_place = (partner_place + 2) % parts
    mesh_id = pl.DeviceIdType.MESH

    def send(src, dst, send_sem, recv_sem, who):
        return pltpu.make_async_remote_copy(
            src_ref=src,
            dst_ref=dst,
            send_sem=send_sem,
            recv_sem=recv_sem,
            device_id={"chan": who},
            device_id_type=mesh_id,
        )

    pairs_in = [
        (own_in, own_ref),
        (mask_in, mask_ref),
        (bank_in, bank_ref),
        (index_in, index_ref),
        (offset_in, offset_ref),
        (owner_in, owner_ref),
    ]
    inputs = [
        pltpu.make_async_copy(src, dst, in_sems.at[n]) for n, (src, dst) in enumerate(pairs_in)
    ]
    for copy in inputs:
        copy.start()

    barrier = pltpu.get_barrier_semaphore()
    partners = [(place != j, base + j) for j in range(parts)]
    for j in range(parts):
        near = jnp.logical_or(place == j, jnp.logical_or(place == parts - 1, j == 0))
        partners.append((jnp.logical_and(row < rows - 1, near), base + parts + j))
        near = jnp.logical_or(place == j, jnp.logical_or(place == 0, j == parts - 1))
        partners.append((jnp.logical_and(row > 0, near), base - parts + j))
    expected = jnp.int32(0)
    for there, who in partners:
        expected += there.astype(jnp.int32)

        @pl.when(there)
        def _(who=who):
            pl.semaphore_signal(barrier, inc=1, device_id={"chan": who}, device_id_type=mesh_id)

    pl.semaphore_wait(barrier, expected)

    peers = [alike_place, corner_place, partner_place]

    def raw_copy(q, to, slot, n, who):
        return send(
            own_ref.at[:, to, :, q * span : (q + 1) * span],
            raw.at[q, slot],
            raw_send.at[min(n // (parts - 1), 1)],
            raw_recv.at[q],
            who,
        )

    def mask_copy(n):
        return send(
            mask_ref, masks.at[place], mask_sems.at[0], mask_sems.at[1], base + peers[n]
        )

    above = jnp.logical_and(place == parts - 1, row < rows - 1)
    below = jnp.logical_and(place == 0, row > 0)

    def edges(q, act):
        @pl.when(above)
        def _():
            for j in range(parts):
                act(raw_copy(q, j, 0, parts - 1 + j, base + parts + j))

        @pl.when(below)
        def _():
            for j in range(parts):
                act(raw_copy(q, j, parts + 1, parts - 1 + j, base - parts + j))

    for copy in inputs:
        copy.wait()
    for n in range(parts - 1):
        mask_copy(n).start()
    for q in range(halves):
        for n in range(2):
            raw_copy(q, peers[n], 1 + place, n, base + peers[n]).start()
        edges(q, lambda copy: copy.start())
        raw_copy(q, peers[2], 1 + place, 2, base + peers[2]).start()

    masks[place] = mask_ref[...]
    for q in range(halves):
        raw[q, 1 + place] = own_ref[:, place, :, q * span : (q + 1) * span]

    @pl.when(row == 0)
    def _():
        raw[:, 0] = jnp.zeros_like(raw[:, 0])

    @pl.when(row == rows - 1)
    def _():
        raw[:, parts + 1] = jnp.zeros_like(raw[:, parts + 1])

    line = Chain(row, rows, lambda i: i * parts + place, HOP, (*line_buf, line_sems))
    line.clear()
    build_bank(bank_ref, toep)
    build_band(band)
    edge = jnp.zeros((power.shape[0], LANES), bf16)
    power[:, :LANES] = edge
    power[:, (cuts + 1) * LANES :] = edge

    def whole(ref, send_sem, recv_sem):
        return send(ref, ref, send_sem, recv_sem, partner)

    whole(masks.at[: parts - 1], mask_sems.at[0], mask_sems.at[1]).wait_recv()
    build_pick(base, place, owner_ref, offset_ref, masks, pick)

    some = back.at[:, : parts - 1]
    count = line.count
    last = HOP * (rows - 1)

    def give(src, dst, n, k, who):
        return send(src.at[k], dst, give_sems.at[n], give_recv.at[(n + 1) // 2, k], who)

    def put(k, j, value):
        src_ref[k, j] = value.astype(f32) * (1.0 / wins)

    def tick(t):
        line.tick(t)
        k = t - last

        @pl.when(jnp.logical_and(k >= 0, k < count))
        def _():
            total = line.result(k)
            done[k] = total
            give(done, across.at[k], 0, k, alike).start()
            give(done, beside.at[k, 0], 1, k, partner).start()
            put(k, place, total)

        q = t - last - SIDE

        @pl.when(jnp.logical_and(q >= 0, q < count))
        def _():
            give(done, across.at[q], 0, q, alike).wait_recv()
            give(across, beside.at[q, 1], 2, q, partner).start()
            put(q, alike_place, across[q])

        b = t - last - SIDE - NEAR

        @pl.when(jnp.logical_and(b >= 0, b < count))
        def _():
            whole(beside.at[b], give_sems.at[1], give_recv.at[1, b]).wait_recv()
            put(b, partner_place, beside[b, 0])
            put(b, corner_place, beside[b, 1])

        @pl.when(b == 0)
        def _():
            whole(some, back_sems.at[0], back_sems.at[1]).wait_recv()
            loc_ref[...] = back[...]

        @pl.when(jnp.logical_and(b >= 0, b < count - LATE))
        def _():
            at, r = b // rounds, b % rounds
            cut = pl.ds(pl.multiple_of(at * LANES, LANES), LANES)
            loc = [[back[at, w, p] for w in range(wins)] for p in range(2)]

            def wide(w, p, j):
                return src_ref[b, w, p, pl.ds(j, 1), :]

            def keep(j, real, imag):
                part_ref[0, r * chans + j, :, cut] = real
                part_ref[1, r * chans + j, :, cut] = imag

            products(wide, loc, keep, chans)

    def back_copy(q, n):
        return send(
            mine.at[q, peers[n]],
            back.at[q, place],
            back_sems.at[0],
            back_sems.at[1],
            base + peers[n],
        )

    def pass_on(q):
        back[q, place] = mine[q, place]

        @pl.loop(q * rounds, (q + 1) * rounds)
        def _(t):
            if last < count:
                tick(t)
            else:
                line.tick(t)

        for n in range(parts - 1):
            back_copy(q, n).start()

    def finish(q):
        whiten_cut(q, band, pick, filt, power, line.own, mine)
        pass_on(q)

    inner = jnp.logical_and(row > 0, row < rows - 1)
    outer = jnp.logical_or(row == 0, row == rows - 1)
    half = cuts // halves
    for first in range(0, cuts, half):
        for there, many in ((inner, parts + 1), (outer, parts)):

            @pl.when(there)
            def _(q=first // half, many=many):
                whole(raw.at[q, :many], raw_send.at[0], raw_recv.at[q]).wait_recv()

        filter_cuts(first, half, nbank, raw, toep, index_ref, filt, power)
        if first == 0:
            for q in range(half - 1):
                finish(q)
    for q in range(half - 1, cuts):
        whiten_cut(q, band, pick, filt, power, line.own, mine)
    for q in range(half - 1, cuts):
        pass_on(q)

    @pl.loop(cuts * rounds, count + last + SIDE + NEAR)
    def _(t):
        tick(t)

    whole(some, back_sems.at[0], back_sems.at[1]).wait_send()
    whole(masks.at[: parts - 1], mask_sems.at[0], mask_sems.at[1]).wait_send()
    whole(raw.at[:, : parts - 1], raw_send.at[0], raw_recv.at[0]).wait_send()

    @pl.when(jnp.logical_or(above, below))
    def _():
        whole(raw.at[:, :parts], raw_send.at[1], raw_recv.at[0]).wait_send()

    line.drain(partner)
    for n in range(3):
        whole(done, give_sems.at[n], give_recv.at[0, 0]).wait_send()


def row_front(rows, owner, own, bank, index, mask, offset):
    _, wins, chans, bins = own.shape
    nbank = bank.shape[1]
    rounds = owner.shape[0]
    cuts = bins // LANES
    parts = wins
    count = cuts * rounds
    outs = LANES // 2
    vmem = pl.BlockSpec(memory_space=pltpu.VMEM)
    chunk = (2, chans, LANES)
    chunks = pltpu.VMEM((count, *chunk), bf16)
    return pl.pallas_call(
        functools.partial(row_kernel, rows),
        out_shape=[
            pltpu.VMEM((cuts, wins, *chunk), bf16),
            pltpu.VMEM((count, wins, *chunk), f32),
            pltpu.VMEM((2, rounds * chans, chans, bins), bf16),
        ],
        in_specs=[pl.BlockSpec(memory_space=pltpu.HBM)] * 6,
        out_specs=[vmem] * 3,
        scratch_shapes=[
            pltpu.SMEM(owner.shape, owner.dtype),
            *[pltpu.VMEM(a.shape, a.dtype) for a in (own, bank, index, mask, offset)],
            pltpu.SemaphoreType.DMA((6,)),
            pltpu.VMEM((2, parts + 2, 2, chans, bins // 2), bf16),
            pltpu.VMEM((parts, wins, chans), jnp.int32),
            pltpu.VMEM((nbank * 2 * outs, 4 * LANES), bf16),
            pltpu.VMEM((3 * LANES, LANES), bf16),
            pltpu.VMEM(((rounds + parts) * chans, parts * chans), bf16),
            pltpu.VMEM((cuts, 2, parts * chans, LANES), f32),
            pltpu.VMEM((parts * chans, (cuts + 2) * LANES), bf16),
            pltpu.VMEM((cuts, parts, *chunk), bf16),
            pltpu.VMEM((cuts, parts, *chunk), bf16),
            [chunks] * 5,
            chunks,
            chunks,
            pltpu.VMEM((count, 2, *chunk), bf16),
            pltpu.SemaphoreType.DMA((2,)),
            pltpu.SemaphoreType.DMA((2,)),
            pltpu.SemaphoreType.DMA((2,)),
            pltpu.SemaphoreType.DMA((2,)),
            pltpu.SemaphoreType.DMA((2, count + 1)),
            pltpu.SemaphoreType.DMA((3,)),
            pltpu.SemaphoreType.DMA((2, count)),
        ],
        compiler_params=pltpu.CompilerParams(
            collective_id=0, has_side_effects=True, vmem_limit_bytes=24 << 20
        ),
        name="front",
    )(*[pltpu.with_memory_space_constraint(a, pltpu.HBM) for a in (owner, own, bank, index, mask, offset)])


def products(wide, loc, put, count):
    wins = len(loc[0])
    chans = loc[0][0].shape[0]

    def one(j, carry):
        src = [
            [
                jnp.broadcast_to(wide(w, p, j), (chans, LANES)).astype(bf16)
                for w in range(wins)
            ]
            for p in range(2)
        ]
        real = tree_sum([src[p][w] * loc[p][w] for w in range(wins) for p in range(2)])
        plus = tree_sum([src[0][w] * loc[1][w] for w in range(wins)])
        minus = tree_sum([src[1][w] * loc[0][w] for w in range(wins)])
        put(j, real, plus - minus)
        return carry

    lax.fori_loop(0, count, one, 0, unroll=16)


def pairs_kernel(src_ref, loc_ref, part_ref, out_ref, buf, sems):
    cuts, wins, _, chans, _ = loc_ref.shape
    count = src_ref.shape[0]
    rounds = count // cuts
    first = count - buf.shape[0]

    def place_of(k, many=1):
        q, r = k // rounds, k % rounds
        rows = slice(r * chans, (r + many) * chans)
        return (slice(None), rows, slice(None), slice(q * LANES, (q + 1) * LANES))

    copies = []
    for k in range(0, first, rounds):
        at = place_of(k, min(rounds, first - k))
        copies.append(
            pltpu.make_async_copy(part_ref.at[at], out_ref.at[at], sems.at[len(copies)])
        )
        copies[-1].start()
    for k in range(first, count):
        loc = [[loc_ref[k // rounds, w, p] for w in range(wins)] for p in range(2)]

        def wide(w, p, j, k=k):
            return src_ref[k, w, p, pl.ds(j, 1), :]

        def put(j, real, imag, k=k):
            buf[k - first, 0, j] = real
            buf[k - first, 1, j] = imag

        products(wide, loc, put, chans)
        copies.append(
            pltpu.make_async_copy(
                buf.at[k - first], out_ref.at[place_of(k)], sems.at[len(copies)]
            )
        )
        copies[-1].start()
    for copy in copies:
        copy.wait()


def pairs(src, loc, part):
    cuts, _, _, chans, _ = loc.shape
    count = src.shape[0]
    late = min(LATE, count)
    vmem = pl.BlockSpec(memory_space=pltpu.VMEM)
    return pl.pallas_call(
        pairs_kernel,
        out_shape=jax.ShapeDtypeStruct(part.shape, bf16),
        in_specs=[vmem] * 3,
        out_specs=pl.BlockSpec(memory_space=pl.ANY),
        scratch_shapes=[
            pltpu.VMEM((late, 2, chans, chans, LANES), bf16),
            pltpu.SemaphoreType.DMA((cuts + late,)),
        ],
        compiler_params=pltpu.CompilerParams(vmem_limit_bytes=16 << 20),
        name="pairs",
    )(src, loc, part)


def body(spectra, filter_bank, band_index, window_mask, owner_order, source_offset):
    grid = chip_grid(lax.axis_size("chan"))
    _, wins, chans, bins = spectra.shape
    ntap = filter_bank.shape[2]
    if 2 * grid[1] == wins == 4 and 4 * chans == LANES and ntap == 2 * chans + 1:
        whitened, sources, part = row_front(
            grid[0],
            owner_order,
            spectra,
            filter_bank,
            band_index[None, :],
            window_mask,
            source_offset,
        )
        return pairs(sources, whitened, part)
    whitened, sources = front(
        grid, owner_order, spectra, filter_bank, band_index[None, :], window_mask
    )
    sources = sources.reshape(sources.shape[0], wins, 2, chans, bins)
    return cross(source_offset, sources, whitened)


def solution(mesh):
    in_specs = (
        P(None, "groups", "chan", None),
        P(),
        P(),
        P("groups", "chan"),
        P("groups"),
        P("groups", None),
    )
    out_specs = P(None, "groups", "chan", None)
    return jax.shard_map(body, mesh=mesh, in_specs=in_specs, out_specs=out_specs, check_vma=False)
```

```python
import functools

import jax
import jax.numpy as jnp
from jax import lax
from jax.experimental import pallas as pl
from jax.experimental.pallas import tpu as pltpu
from jax.sharding import PartitionSpec as P

SMOOTH = 17
water_level = 0.05
bf16 = jnp.bfloat16
f32 = jnp.float32
LANES = 128
LAG = 4


def split(x):
    hi = x.astype(bf16)
    return hi, (x - hi.astype(f32)).astype(bf16)


def build_toeplitz(bank_ref, toep):
    _, nbank, ntap = bank_ref.shape
    chans = toep.shape[1] // (2 * nbank)
    for b in range(nbank):
        parts = []
        for p in range(2):
            row = jnp.concatenate(
                [bank_ref[p, b : b + 1, :], jnp.zeros((1, LANES - ntap), f32)], axis=1
            )
            full = jnp.broadcast_to(row, (chans, LANES))
            parts.append(split(pltpu.roll(full, 0, 1, stride=1, stride_axis=0)))
        at = b * 2 * chans
        for part in range(2):
            real, imag = parts[0][part], parts[1][part]
            toep[part, at : at + chans, :LANES] = real
            toep[part, at : at + chans, LANES:] = -imag
            toep[part, at + chans : at + 2 * chans, :LANES] = imag
            toep[part, at + chans : at + 2 * chans, LANES:] = real


def build_window(band):
    bins = band.shape[0]
    rows = lax.broadcasted_iota(jnp.int32, (bins, bins), 0)
    cols = lax.broadcasted_iota(jnp.int32, (bins, bins), 1)
    band[...] = (jnp.abs(rows - cols) <= SMOOTH // 2).astype(f32).astype(bf16)


def filter_window(nbank, w, x, toep, index_ref, filt, power):
    bins = filt.shape[2]
    chans = toep.shape[1] // (2 * nbank)
    tile = 256
    rows = slice(w * chans, (w + 1) * chans)
    for n in range(bins // tile):
        cut = slice(n * tile, (n + 1) * tile)
        here = x(cut)
        res = jnp.dot(toep[0], here, preferred_element_type=f32)
        res += jnp.dot(toep[1], here, preferred_element_type=f32)
        index = index_ref[:, cut]
        acc = res[: 2 * chans]
        for b in range(1, nbank):
            acc = jnp.where(index == b, res[2 * chans * b : 2 * chans * (b + 1)], acc)
        real, imag = acc[:chans], acc[chans:]
        filt[0, rows, cut] = real
        filt[1, rows, cut] = imag
        hi, lo = split(real * real + imag * imag)
        power[0, rows, cut] = hi
        power[1, rows, cut] = lo


def whiten_window(w, band, mask_ref, filt, power):
    chans = mask_ref.shape[1]
    rows = slice(w * chans, (w + 1) * chans)
    smooth = jnp.dot(power[0, rows], band[...], preferred_element_type=f32)
    smooth += jnp.dot(power[1, rows], band[...], preferred_element_type=f32)
    scale = lax.rsqrt(smooth * (1.0 / SMOOTH) + water_level)
    eye = lax.broadcasted_iota(jnp.int32, (chans, chans), 0) == lax.broadcasted_iota(
        jnp.int32, (chans, chans), 1
    )
    row = jnp.broadcast_to(mask_ref[w : w + 1, :].astype(f32), (chans, chans))
    valid = jnp.sum(jnp.where(eye, row, 0.0), axis=1, keepdims=True)
    scale = scale * valid
    return [(filt[p, rows] * scale).astype(bf16) for p in range(2)]


class Line:
    def __init__(self, pos, length, device_of, lag, refs):
        self.pos, self.length, self.device_of, self.lag = pos, length, device_of, lag
        self.own, self.out_r, self.out_l, self.in_r, self.in_l, self.sems = refs
        self.count = self.own.shape[0]

    def clear(self):
        @pl.when(self.pos == 0)
        def _():
            self.in_r[...] = jnp.zeros_like(self.in_r)

        @pl.when(self.pos == self.length - 1)
        def _():
            self.in_l[...] = jnp.zeros_like(self.in_l)

    def copy(self, way, k):
        out, into = (self.out_r, self.in_r) if way == 0 else (self.out_l, self.in_l)
        other = self.pos + 1 if way == 0 else self.pos - 1
        return pltpu.make_async_remote_copy(
            src_ref=out.at[k],
            dst_ref=into.at[k],
            send_sem=self.sems.at[way, 0, k],
            recv_sem=self.sems.at[way, 1, k],
            device_id={"chan": self.device_of(other)},
            device_id_type=pl.DeviceIdType.MESH,
        )

    def tick(self, t):
        for way in range(2):
            behind = self.pos if way == 0 else self.length - 1 - self.pos
            out, into = (self.out_r, self.in_r) if way == 0 else (self.out_l, self.in_l)
            k = t - self.lag * behind
            inside = jnp.logical_and(k >= 0, k < self.count)

            @pl.when(jnp.logical_and(inside, behind > 0))
            def _(way=way, k=k):
                self.copy(way, k).wait_recv()

            @pl.when(jnp.logical_and(inside, behind < self.length - 1))
            def _(way=way, k=k, out=out, into=into):
                out[k] = self.own[k] + into[k]
                self.copy(way, k).start()

    def result(self, k):
        return self.own[k] + self.in_r[k] + self.in_l[k]

    def drain(self):
        for way in range(2):
            behind = self.pos if way == 0 else self.length - 1 - self.pos

            @pl.when(behind < self.length - 1)
            def _(way=way):
                @pl.loop(0, self.count)
                def _(k):
                    self.copy(way, k).wait_send()


def front_kernel(
    rows,
    cols,
    owner_ref,
    own_ref,
    bank_ref,
    index_ref,
    mask_ref,
    out_ref,
    src_ref,
    halo,
    toep,
    band,
    filt,
    power,
    mine,
    beside,
    row_buf,
    done,
    gathered,
    halo_sems,
    beside_sems,
    row_sems,
    gather_sems,
):
    wins, chans = mask_ref.shape
    bins = own_ref.shape[3]
    parts = 2 * cols
    subs, piece = beside.shape[1], beside.shape[2]
    me = lax.axis_index("chan")
    size = rows * cols * 2
    core = me % 2
    place = me % (2 * cols)
    base = me - place
    row = me // (2 * cols)
    partner = me + 1 - 2 * core
    mesh_id = pl.DeviceIdType.MESH

    barrier = pltpu.get_barrier_semaphore()
    partners = [
        (me > 0, me - 1),
        (me < size - 1, me + 1),
        (row > 0, me - 2 * cols),
        (row < rows - 1, me + 2 * cols),
    ] + [(place != j, base + j) for j in range(2 * cols)]
    expected = jnp.int32(0)
    for there, who in partners:
        expected += there.astype(jnp.int32)

        @pl.when(there)
        def _(who=who):
            pl.semaphore_signal(barrier, inc=1, device_id={"chan": who}, device_id_type=mesh_id)

    pl.semaphore_wait(barrier, expected)

    def halo_copy(way, w):
        return pltpu.make_async_remote_copy(
            src_ref=own_ref.at[:, w],
            dst_ref=halo.at[way, :, w],
            send_sem=halo_sems.at[way, 0, w],
            recv_sem=halo_sems.at[way, 1, w],
            device_id={"chan": me + 1 - 2 * way},
            device_id_type=mesh_id,
        )

    order = list(range(wins))
    sends = (me < size - 1, me > 0)
    for w in order:
        for way in range(2):

            @pl.when(sends[way])
            def _(way=way, w=w):
                halo_copy(way, w).start()

    for way in range(2):

        @pl.when(jnp.logical_not(sends[1 - way]))
        def _(way=way):
            halo[way] = jnp.zeros_like(halo[way])

    line = Line(row, rows, lambda i: i * 2 * cols + place, LAG, (*row_buf, row_sems))
    line.clear()
    build_toeplitz(bank_ref, toep)
    build_window(band)

    def beside_copy(sender, j):
        return pltpu.make_async_remote_copy(
            src_ref=mine.at[pl.ds(j * subs, subs)],
            dst_ref=beside.at[sender],
            send_sem=beside_sems.at[0, j],
            recv_sem=beside_sems.at[1, sender],
            device_id={"chan": base + j},
            device_id_type=mesh_id,
        )

    blank = jnp.zeros((LANES - 3 * chans, bins), bf16)
    for w in order:
        for way in range(2):

            @pl.when(sends[1 - way])
            def _(way=way, w=w):
                halo_copy(way, w).wait_recv()

        def x(cut, w=w):
            stack = []
            for p in range(2):
                stack += [halo[0, p, w, :, cut], own_ref[p, w, :, cut], halo[1, p, w, :, cut]]
                stack += [blank[:, cut]]
            return jnp.concatenate(stack, axis=0)

        filter_window(bank_ref.shape[1], w, x, toep, index_ref, filt, power)
        white = whiten_window(w, band, mask_ref, filt, power)
        for p in range(2):
            out_ref[p, w] = white[p]
            for i in range(chans // piece):
                mine[(w * 2 + p) * (chans // piece) + i] = white[p][i * piece : (i + 1) * piece]
        for j in range(w * parts // wins, (w + 1) * parts // wins):

            @pl.when(place != j)
            def _(j=j):
                beside_copy(place, j).start()

    beside[place] = mine[pl.ds(place * subs, subs)]
    for j in range(parts):

        @pl.when(place != j)
        def _(j=j):
            beside_copy(j, j).wait_recv()

    count = line.count

    @pl.loop(0, count)
    def _(k):
        total = jnp.zeros((piece, bins), bf16)
        for j in range(parts):
            total += beside[j, k % subs] * (owner_ref[k // subs] == base + j).astype(f32).astype(bf16)
        line.own[k] = total

    def give(src, origin, k, sem, who):
        return pltpu.make_async_remote_copy(
            src_ref=src,
            dst_ref=gathered.at[origin, k],
            send_sem=gather_sems.at[sem, k],
            recv_sem=gather_sems.at[2 * parts + origin, k],
            device_id={"chan": who},
            device_id_type=mesh_id,
        )

    def put(j, k, value):
        src_ref[k // subs, j * subs + k % subs] = value

    alike = [jnp.logical_and(place != j, core == j % 2) for j in range(parts)]
    last = LAG * (rows - 1)

    @pl.loop(0, count + last + LAG)
    def _(t):
        line.tick(t)
        k = t - last

        @pl.when(jnp.logical_and(k >= 0, k < count))
        def _():
            total = line.result(k)
            done[k] = total
            for j in range(parts):

                @pl.when(alike[j])
                def _(j=j):
                    give(done.at[k], place, k, j, base + j).start()

            give(done.at[k], place, k, parts + place, partner).start()
            put(place, k, total)

        q = t - last - LAG

        @pl.when(q >= 0)
        def _():
            for j in range(parts):

                @pl.when(alike[j])
                def _(j=j):
                    give(done.at[q], j, q, j, partner).wait_recv()
                    give(gathered.at[j, q], j, q, parts + j, partner).start()
                    put(j, q, gathered[j, q])

    @pl.loop(0, count)
    def _(k):
        for j in range(parts):

            @pl.when(core != j % 2)
            def _(j=j):
                give(done.at[k], j, k, j, partner).wait_recv()
                put(j, k, gathered[j, k])

    for way in range(2):
        for w in range(wins):

            @pl.when(sends[way])
            def _(way=way, w=w):
                halo_copy(way, w).wait_send()

    for j in range(parts):

        @pl.when(place != j)
        def _(j=j):
            beside_copy(place, j).wait_send()

    line.drain()

    @pl.loop(0, count)
    def _(k):
        give(done.at[k], place, k, parts + place, partner).wait_send()
        for j in range(parts):

            @pl.when(alike[j])
            def _(j=j):
                give(done.at[k], place, k, j, partner).wait_send()
                give(gathered.at[j, k], j, k, parts + j, partner).wait_send()


def front(grid, owner, own, bank, index, mask):
    _, wins, chans, bins = own.shape
    nbank = bank.shape[1]
    rounds = owner.shape[0]
    rows, cols = grid
    parts = 2 * cols
    total = wins * 2 * chans
    piece = min(chans, total // parts)
    subs = total // parts // piece
    count = rounds * subs
    vmem = pl.BlockSpec(memory_space=pltpu.VMEM)
    chunk = (piece, bins)
    chunks = pltpu.VMEM((count, *chunk), bf16)
    return pl.pallas_call(
        functools.partial(front_kernel, rows, cols),
        out_shape=[
            jax.ShapeDtypeStruct(own.shape, bf16),
            jax.ShapeDtypeStruct((rounds, parts * subs, piece, bins), bf16),
        ],
        in_specs=[pl.BlockSpec(memory_space=pltpu.SMEM)] + [vmem] * 4,
        out_specs=[vmem] * 2,
        scratch_shapes=[
            pltpu.VMEM((2, *own.shape), bf16),
            pltpu.VMEM((2, nbank * 2 * chans, 2 * LANES), bf16),
            pltpu.VMEM((bins, bins), bf16),
            pltpu.VMEM((2, wins * chans, bins), f32),
            pltpu.VMEM((2, wins * chans, bins), bf16),
            pltpu.VMEM((parts * subs, *chunk), bf16),
            pltpu.VMEM((parts, subs, *chunk), bf16),
            [chunks] * 5,
            chunks,
            pltpu.VMEM((parts, count, *chunk), bf16),
            pltpu.SemaphoreType.DMA((2, 2, wins)),
            pltpu.SemaphoreType.DMA((2, parts)),
            pltpu.SemaphoreType.DMA((2, 2, count)),
            pltpu.SemaphoreType.DMA((3 * parts, count)),
        ],
        compiler_params=pltpu.CompilerParams(collective_id=0, has_side_effects=True),
        name="front",
    )(owner, own, bank, index, mask)


def tree_sum(terms):
    while len(terms) > 1:
        terms = [a + b for a, b in zip(terms[::2], terms[1::2])]
    return terms[0]


def cross_kernel(offset_ref, src_ref, loc_ref, out_ref, wide, held):
    _, wins, chans, bins = loc_ref.shape
    count = out_ref.shape[1]
    r, h = pl.program_id(0), pl.program_id(1)

    @pl.when(jnp.logical_and(r == 0, h == 0))
    def _():
        held[...] = loc_ref[...]

    @pl.when(h == 0)
    def _():
        for p in range(2):
            for w in range(wins):
                wide[:, p * wins + w, :] = src_ref[0, w, p].astype(f32) * (1.0 / wins)

    for n in range(bins // LANES):
        cut = slice(n * LANES, (n + 1) * LANES)

        def one(j, carry, cut=cut):
            loc = [[held[p, w, :, cut] for w in range(wins)] for p in range(2)]
            at = offset_ref[r, h * count + j]
            src = [
                [
                    jnp.broadcast_to(
                        wide[at, p * wins + w : p * wins + w + 1, cut], (chans, LANES)
                    ).astype(bf16)
                    for w in range(wins)
                ]
                for p in range(2)
            ]
            real = tree_sum(
                [src[p][w] * loc[p][w] for w in range(wins) for p in range(2)]
            )
            plus = tree_sum([src[0][w] * loc[1][w] for w in range(wins)])
            minus = tree_sum([src[1][w] * loc[0][w] for w in range(wins)])
            out_ref[0, j, :, cut] = real
            out_ref[1, j, :, cut] = plus - minus
            return carry

        lax.fori_loop(0, count, one, 0, unroll=4)


def cross(offset, src, loc, blocks=1):
    rounds, wins, _, chans, bins = src.shape
    per = chans // blocks
    return pl.pallas_call(
        cross_kernel,
        out_shape=jax.ShapeDtypeStruct((2, rounds * chans, chans, bins), bf16),
        grid=(rounds, blocks),
        in_specs=[
            pl.BlockSpec(memory_space=pltpu.SMEM),
            pl.BlockSpec((1, wins, 2, chans, bins), lambda r, h: (r, 0, 0, 0, 0)),
            pl.BlockSpec((2, wins, chans, bins), lambda r, h: (0, 0, 0, 0)),
        ],
        out_specs=pl.BlockSpec((2, per, chans, bins), lambda r, h: (0, r * blocks + h, 0, 0)),
        scratch_shapes=[
            pltpu.VMEM((chans, 2 * wins, bins), f32),
            pltpu.VMEM((2, wins, chans, bins), bf16),
        ],
        name="cross",
    )(offset, src, loc)


def chip_grid(size):
    chips = size // 2
    cols = 1
    while cols * cols * 4 <= chips:
        cols *= 2
    return chips // cols, cols


HOP, SIDE, NEAR, LATE = 8, 8, 4, 7


class Chain(Line):
    def copy(self, way, k):
        out, into = (self.out_r, self.in_r) if way == 0 else (self.out_l, self.in_l)
        other = self.pos + 1 if way == 0 else self.pos - 1
        return self.make(way, out.at[k], into.at[k], k, self.device_of(other))

    def make(self, way, src, dst, k, who):
        return pltpu.make_async_remote_copy(
            src_ref=src,
            dst_ref=dst,
            send_sem=self.sems.at[way, self.count],
            recv_sem=self.sems.at[way, k],
            device_id={"chan": who},
            device_id_type=pl.DeviceIdType.MESH,
        )

    def drain(self, who):
        for way in range(2):
            behind = self.pos if way == 0 else self.length - 1 - self.pos
            out = self.out_r if way == 0 else self.out_l

            @pl.when(behind < self.length - 1)
            def _(way=way, out=out):
                self.make(way, out, out, 0, who).wait_send()


def build_bank(bank_ref, toep):
    _, nbank, ntap = bank_ref.shape
    outs = toep.shape[0] // (2 * nbank)
    for b in range(nbank):
        parts = []
        for p in range(2):
            row = jnp.concatenate(
                [bank_ref[p, b : b + 1, :], jnp.zeros((1, LANES - ntap), f32)], axis=1
            )
            full = jnp.broadcast_to(row, (outs, LANES))
            parts.append(split(pltpu.roll(full, 0, 1, stride=1, stride_axis=0)))
        at = b * 2 * outs
        for part in range(2):
            real, imag = parts[0][part], parts[1][part]
            left = slice(2 * part * LANES, (2 * part + 1) * LANES)
            right = slice((2 * part + 1) * LANES, (2 * part + 2) * LANES)
            toep[at : at + outs, left] = real
            toep[at : at + outs, right] = -imag
            toep[at + outs : at + 2 * outs, left] = imag
            toep[at + outs : at + 2 * outs, right] = real


def build_band(band):
    wide, bins = band.shape
    rows = lax.broadcasted_iota(jnp.int32, (wide, bins), 0)
    cols = lax.broadcasted_iota(jnp.int32, (wide, bins), 1)
    band[...] = (jnp.abs(rows - bins - cols) <= SMOOTH // 2).astype(f32).astype(bf16)


def build_pick(base, place, owner_ref, offset_ref, masks, pick):
    parts, _, chans = masks.shape
    rounds = offset_ref.shape[0]
    total = parts * chans
    valid = jnp.concatenate(
        [masks[b, pl.ds(place, 1), :].astype(f32) for b in range(parts)], axis=1
    )
    eye = lax.broadcasted_iota(jnp.int32, (chans, chans), 0) == lax.broadcasted_iota(
        jnp.int32, (chans, chans), 1
    )
    cols = lax.broadcasted_iota(jnp.int32, (chans, total), 1).astype(f32)
    for r in range(rounds):
        row = jnp.broadcast_to(offset_ref[r : r + 1, :].astype(f32), (chans, chans))
        col = jnp.sum(jnp.where(eye, row, 0.0), axis=1, keepdims=True)
        col = col + ((owner_ref[r] - base) * chans).astype(f32)
        pick[r * chans : (r + 1) * chans] = jnp.where(cols == col, valid, 0.0).astype(bf16)
    rows = lax.broadcasted_iota(jnp.int32, (total, total), 0)
    same = rows == lax.broadcasted_iota(jnp.int32, (total, total), 1)
    pick[rounds * chans :] = jnp.where(same, valid, 0.0).astype(bf16)


def filter_cuts(first, cuts, nbank, raw, toep, index_ref, filt, power):
    outs = toep.shape[0] // (2 * nbank)
    blocks, chans = raw.shape[1], raw.shape[3]
    step = outs // chans
    many = range(first, first + cuts)
    index = index_ref[:, first * LANES : (first + cuts) * LANES]
    for u in range((blocks - 2) // step):
        here = [
            raw[first // cuts, u * step : u * step + step + 2, p].reshape(
                (step + 2) * chans, cuts * LANES
            )
            for p in range(2)
        ]
        res = jnp.dot(
            toep[...], jnp.concatenate(here + here, axis=0), preferred_element_type=f32
        )
        acc = res[: 2 * outs]
        for b in range(1, nbank):
            acc = jnp.where(index == b, res[2 * outs * b : 2 * outs * (b + 1)], acc)
        real, imag = acc[:outs], acc[outs:]
        rows = slice(u * outs, (u + 1) * outs)
        for q in many:
            cut = slice((q - first) * LANES, (q - first + 1) * LANES)
            filt[q, 0, rows] = real[:, cut]
            filt[q, 1, rows] = imag[:, cut]
        power[rows, (first + 1) * LANES : (first + cuts + 1) * LANES] = (
            real * real + imag * imag
        ).astype(bf16)


def whiten_cut(q, band, pick, filt, power, own, mine):
    rounds = own.shape[0] // filt.shape[0]
    chans = own.shape[2]
    smooth = jnp.dot(
        power[:, q * LANES : (q + 3) * LANES], band[...], preferred_element_type=f32
    )
    scale = lax.rsqrt(smooth * (1.0 / SMOOTH) + water_level)
    white = jnp.concatenate([(filt[q, p] * scale).astype(bf16) for p in range(2)], axis=1)
    res = jnp.dot(pick[...], white, preferred_element_type=f32).astype(bf16)
    at = rounds * chans
    for p in range(2):
        cut = slice(p * LANES, (p + 1) * LANES)
        for r in range(rounds):
            own[q * rounds + r, p] = res[r * chans : (r + 1) * chans, cut]
        for b in range(mine.shape[1]):
            mine[q, b, p] = res[at + b * chans : at + (b + 1) * chans, cut]


def row_kernel(
    rows,
    owner_in,
    own_in,
    bank_in,
    index_in,
    mask_in,
    offset_in,
    loc_ref,
    src_ref,
    part_ref,
    owner_ref,
    own_ref,
    bank_ref,
    index_ref,
    mask_ref,
    offset_ref,
    in_sems,
    raw,
    masks,
    toep,
    band,
    pick,
    filt,
    power,
    mine,
    back,
    line_buf,
    done,
    across,
    beside,
    raw_send,
    raw_recv,
    mask_sems,
    back_sems,
    line_sems,
    give_sems,
    give_recv,
):
    wins, chans = mask_ref.shape
    halves, span = raw.shape[0], raw.shape[4]
    cuts = halves * span // LANES
    nbank = bank_ref.shape[1]
    parts = wins
    rounds = owner_ref.shape[0]
    me = lax.axis_index("chan")
    core = me % 2
    place = me % parts
    base = me - place
    row = me // parts
    partner = me + 1 - 2 * core
    alike = base + (place + 2) % parts
    partner_place = place + 1 - 2 * core
    alike_place = (place + 2) % parts
    corner_place = (partner_place + 2) % parts
    mesh_id = pl.DeviceIdType.MESH

    def send(src, dst, send_sem, recv_sem, who):
        return pltpu.make_async_remote_copy(
            src_ref=src,
            dst_ref=dst,
            send_sem=send_sem,
            recv_sem=recv_sem,
            device_id={"chan": who},
            device_id_type=mesh_id,
        )

    pairs_in = [
        (own_in, own_ref),
        (mask_in, mask_ref),
        (bank_in, bank_ref),
        (index_in, index_ref),
        (offset_in, offset_ref),
        (owner_in, owner_ref),
    ]
    inputs = [
        pltpu.make_async_copy(src, dst, in_sems.at[n]) for n, (src, dst) in enumerate(pairs_in)
    ]
    for copy in inputs:
        copy.start()

    barrier = pltpu.get_barrier_semaphore()
    partners = [(place != j, base + j) for j in range(parts)]
    for j in range(parts):
        near = jnp.logical_or(place == j, jnp.logical_or(place == parts - 1, j == 0))
        partners.append((jnp.logical_and(row < rows - 1, near), base + parts + j))
        near = jnp.logical_or(place == j, jnp.logical_or(place == 0, j == parts - 1))
        partners.append((jnp.logical_and(row > 0, near), base - parts + j))
    expected = jnp.int32(0)
    for there, who in partners:
        expected += there.astype(jnp.int32)

        @pl.when(there)
        def _(who=who):
            pl.semaphore_signal(barrier, inc=1, device_id={"chan": who}, device_id_type=mesh_id)

    pl.semaphore_wait(barrier, expected)

    peers = [alike_place, corner_place, partner_place]

    def raw_copy(q, to, slot, n, who):
        return send(
            own_ref.at[:, to, :, q * span : (q + 1) * span],
            raw.at[q, slot],
            raw_send.at[min(n // (parts - 1), 1)],
            raw_recv.at[q],
            who,
        )

    def mask_copy(n):
        return send(
            mask_ref, masks.at[place], mask_sems.at[0], mask_sems.at[1], base + peers[n]
        )

    above = jnp.logical_and(place == parts - 1, row < rows - 1)
    below = jnp.logical_and(place == 0, row > 0)

    def edges(q, act):
        @pl.when(above)
        def _():
            for j in range(parts):
                act(raw_copy(q, j, 0, parts - 1 + j, base + parts + j))

        @pl.when(below)
        def _():
            for j in range(parts):
                act(raw_copy(q, j, parts + 1, parts - 1 + j, base - parts + j))

    for copy in inputs:
        copy.wait()
    for n in range(parts - 1):
        mask_copy(n).start()
    for q in range(halves):
        for n in range(2):
            raw_copy(q, peers[n], 1 + place, n, base + peers[n]).start()
        edges(q, lambda copy: copy.start())
        raw_copy(q, peers[2], 1 + place, 2, base + peers[2]).start()

    masks[place] = mask_ref[...]
    for q in range(halves):
        raw[q, 1 + place] = own_ref[:, place, :, q * span : (q + 1) * span]

    @pl.when(row == 0)
    def _():
        raw[:, 0] = jnp.zeros_like(raw[:, 0])

    @pl.when(row == rows - 1)
    def _():
        raw[:, parts + 1] = jnp.zeros_like(raw[:, parts + 1])

    line = Chain(row, rows, lambda i: i * parts + place, HOP, (*line_buf, line_sems))
    line.clear()
    build_bank(bank_ref, toep)
    build_band(band)
    edge = jnp.zeros((power.shape[0], LANES), bf16)
    power[:, :LANES] = edge
    power[:, (cuts + 1) * LANES :] = edge

    def whole(ref, send_sem, recv_sem):
        return send(ref, ref, send_sem, recv_sem, partner)

    whole(masks.at[: parts - 1], mask_sems.at[0], mask_sems.at[1]).wait_recv()
    build_pick(base, place, owner_ref, offset_ref, masks, pick)

    some = back.at[:, : parts - 1]
    count = line.count
    last = HOP * (rows - 1)

    def give(src, dst, n, k, who):
        return send(src.at[k], dst, give_sems.at[n], give_recv.at[(n + 1) // 2, k], who)

    def put(k, j, value):
        src_ref[k, j] = value.astype(f32) * (1.0 / wins)

    def tick(t):
        line.tick(t)
        k = t - last

        @pl.when(jnp.logical_and(k >= 0, k < count))
        def _():
            total = line.result(k)
            done[k] = total
            give(done, across.at[k], 0, k, alike).start()
            give(done, beside.at[k, 0], 1, k, partner).start()
            put(k, place, total)

        q = t - last - SIDE

        @pl.when(jnp.logical_and(q >= 0, q < count))
        def _():
            give(done, across.at[q], 0, q, alike).wait_recv()
            give(across, beside.at[q, 1], 2, q, partner).start()
            put(q, alike_place, across[q])

        b = t - last - SIDE - NEAR

        @pl.when(jnp.logical_and(b >= 0, b < count))
        def _():
            whole(beside.at[b], give_sems.at[1], give_recv.at[1, b]).wait_recv()
            put(b, partner_place, beside[b, 0])
            put(b, corner_place, beside[b, 1])

        @pl.when(b == 0)
        def _():
            whole(some, back_sems.at[0], back_sems.at[1]).wait_recv()
            loc_ref[...] = back[...]

        @pl.when(jnp.logical_and(b >= 0, b < count - LATE))
        def _():
            at, r = b // rounds, b % rounds
            cut = pl.ds(pl.multiple_of(at * LANES, LANES), LANES)
            loc = [[back[at, w, p] for w in range(wins)] for p in range(2)]

            def wide(w, p, j):
                return src_ref[b, w, p, pl.ds(j, 1), :]

            def keep(j, real, imag):
                part_ref[0, r * chans + j, :, cut] = real
                part_ref[1, r * chans + j, :, cut] = imag

            products(wide, loc, keep, chans)

    def back_copy(q, n):
        return send(
            mine.at[q, peers[n]],
            back.at[q, place],
            back_sems.at[0],
            back_sems.at[1],
            base + peers[n],
        )

    def pass_on(q):
        back[q, place] = mine[q, place]

        @pl.loop(q * rounds, (q + 1) * rounds)
        def _(t):
            if last < count:
                tick(t)
            else:
                line.tick(t)

        for n in range(parts - 1):
            back_copy(q, n).start()

    def finish(q):
        whiten_cut(q, band, pick, filt, power, line.own, mine)
        pass_on(q)

    inner = jnp.logical_and(row > 0, row < rows - 1)
    outer = jnp.logical_or(row == 0, row == rows - 1)
    half = cuts // halves
    for first in range(0, cuts, half):
        for there, many in ((inner, parts + 1), (outer, parts)):

            @pl.when(there)
            def _(q=first // half, many=many):
                whole(raw.at[q, :many], raw_send.at[0], raw_recv.at[q]).wait_recv()

        filter_cuts(first, half, nbank, raw, toep, index_ref, filt, power)
        if first == 0:
            for q in range(half - 1):
                finish(q)
    for q in range(half - 1, cuts):
        whiten_cut(q, band, pick, filt, power, line.own, mine)
    for q in range(half - 1, cuts):
        pass_on(q)

    @pl.loop(cuts * rounds, count + last + SIDE + NEAR)
    def _(t):
        tick(t)

    whole(some, back_sems.at[0], back_sems.at[1]).wait_send()
    whole(masks.at[: parts - 1], mask_sems.at[0], mask_sems.at[1]).wait_send()
    whole(raw.at[:, : parts - 1], raw_send.at[0], raw_recv.at[0]).wait_send()

    @pl.when(jnp.logical_or(above, below))
    def _():
        whole(raw.at[:, :parts], raw_send.at[1], raw_recv.at[0]).wait_send()

    line.drain(partner)
    for n in range(3):
        whole(done, give_sems.at[n], give_recv.at[0, 0]).wait_send()


def row_front(rows, owner, own, bank, index, mask, offset):
    _, wins, chans, bins = own.shape
    nbank = bank.shape[1]
    rounds = owner.shape[0]
    cuts = bins // LANES
    parts = wins
    count = cuts * rounds
    outs = LANES // 2
    vmem = pl.BlockSpec(memory_space=pltpu.VMEM)
    chunk = (2, chans, LANES)
    chunks = pltpu.VMEM((count, *chunk), bf16)
    return pl.pallas_call(
        functools.partial(row_kernel, rows),
        out_shape=[
            pltpu.VMEM((cuts, wins, *chunk), bf16),
            pltpu.VMEM((count, wins, *chunk), f32),
            pltpu.VMEM((2, rounds * chans, chans, bins), bf16),
        ],
        in_specs=[pl.BlockSpec(memory_space=pltpu.HBM)] * 6,
        out_specs=[vmem] * 3,
        scratch_shapes=[
            pltpu.SMEM(owner.shape, owner.dtype),
            *[pltpu.VMEM(a.shape, a.dtype) for a in (own, bank, index, mask, offset)],
            pltpu.SemaphoreType.DMA((6,)),
            pltpu.VMEM((2, parts + 2, 2, chans, bins // 2), bf16),
            pltpu.VMEM((parts, wins, chans), jnp.int32),
            pltpu.VMEM((nbank * 2 * outs, 4 * LANES), bf16),
            pltpu.VMEM((3 * LANES, LANES), bf16),
            pltpu.VMEM(((rounds + parts) * chans, parts * chans), bf16),
            pltpu.VMEM((cuts, 2, parts * chans, LANES), f32),
            pltpu.VMEM((parts * chans, (cuts + 2) * LANES), bf16),
            pltpu.VMEM((cuts, parts, *chunk), bf16),
            pltpu.VMEM((cuts, parts, *chunk), bf16),
            [chunks] * 5,
            chunks,
            chunks,
            pltpu.VMEM((count, 2, *chunk), bf16),
            pltpu.SemaphoreType.DMA((2,)),
            pltpu.SemaphoreType.DMA((2,)),
            pltpu.SemaphoreType.DMA((2,)),
            pltpu.SemaphoreType.DMA((2,)),
            pltpu.SemaphoreType.DMA((2, count + 1)),
            pltpu.SemaphoreType.DMA((3,)),
            pltpu.SemaphoreType.DMA((2, count)),
        ],
        compiler_params=pltpu.CompilerParams(
            collective_id=0, has_side_effects=True, vmem_limit_bytes=24 << 20
        ),
        name="front",
    )(*[pltpu.with_memory_space_constraint(a, pltpu.HBM) for a in (owner, own, bank, index, mask, offset)])


def products(wide, loc, put, count):
    wins = len(loc[0])
    chans = loc[0][0].shape[0]

    def one(j, carry):
        src = [
            [
                jnp.broadcast_to(wide(w, p, j), (chans, LANES)).astype(bf16)
                for w in range(wins)
            ]
            for p in range(2)
        ]
        real = tree_sum([src[p][w] * loc[p][w] for w in range(wins) for p in range(2)])
        plus = tree_sum([src[0][w] * loc[1][w] for w in range(wins)])
        minus = tree_sum([src[1][w] * loc[0][w] for w in range(wins)])
        put(j, real, plus - minus)
        return carry

    lax.fori_loop(0, count, one, 0, unroll=32)


def pairs_kernel(src_ref, loc_ref, part_ref, out_ref, buf, sems):
    cuts, wins, _, chans, _ = loc_ref.shape
    count = src_ref.shape[0]
    rounds = count // cuts
    first = count - buf.shape[0]

    def place_of(k, many=1):
        q, r = k // rounds, k % rounds
        rows = slice(r * chans, (r + many) * chans)
        return (slice(None), rows, slice(None), slice(q * LANES, (q + 1) * LANES))

    copies = []
    for k in range(0, first, rounds):
        at = place_of(k, min(rounds, first - k))
        copies.append(
            pltpu.make_async_copy(part_ref.at[at], out_ref.at[at], sems.at[len(copies)])
        )
        copies[-1].start()
    for k in range(first, count):
        loc = [[loc_ref[k // rounds, w, p] for w in range(wins)] for p in range(2)]

        def wide(w, p, j, k=k):
            return src_ref[k, w, p, pl.ds(j, 1), :]

        def put(j, real, imag, k=k):
            buf[k - first, 0, j] = real
            buf[k - first, 1, j] = imag

        products(wide, loc, put, chans)
        copies.append(
            pltpu.make_async_copy(
                buf.at[k - first], out_ref.at[place_of(k)], sems.at[len(copies)]
            )
        )
        copies[-1].start()
    for copy in copies:
        copy.wait()


def pairs(src, loc, part):
    cuts, _, _, chans, _ = loc.shape
    count = src.shape[0]
    late = min(LATE, count)
    vmem = pl.BlockSpec(memory_space=pltpu.VMEM)
    return pl.pallas_call(
        pairs_kernel,
        out_shape=jax.ShapeDtypeStruct(part.shape, bf16),
        in_specs=[vmem] * 3,
        out_specs=pl.BlockSpec(memory_space=pl.ANY),
        scratch_shapes=[
            pltpu.VMEM((late, 2, chans, chans, LANES), bf16),
            pltpu.SemaphoreType.DMA((cuts + late,)),
        ],
        compiler_params=pltpu.CompilerParams(vmem_limit_bytes=16 << 20),
        name="pairs",
    )(src, loc, part)


def body(spectra, filter_bank, band_index, window_mask, owner_order, source_offset):
    grid = chip_grid(lax.axis_size("chan"))
    _, wins, chans, bins = spectra.shape
    ntap = filter_bank.shape[2]
    if 2 * grid[1] == wins == 4 and 4 * chans == LANES and ntap == 2 * chans + 1:
        whitened, sources, part = row_front(
            grid[0],
            owner_order,
            spectra,
            filter_bank,
            band_index[None, :],
            window_mask,
            source_offset,
        )
        return pairs(sources, whitened, part)
    whitened, sources = front(
        grid, owner_order, spectra, filter_bank, band_index[None, :], window_mask
    )
    sources = sources.reshape(sources.shape[0], wins, 2, chans, bins)
    return cross(source_offset, sources, whitened)


def solution(mesh):
    in_specs = (
        P(None, "groups", "chan", None),
        P(),
        P(),
        P("groups", "chan"),
        P("groups"),
        P("groups", None),
    )
    out_specs = P(None, "groups", "chan", None)
    return jax.shard_map(body, mesh=mesh, in_specs=in_specs, out_specs=out_specs, check_vma=False)
```

```python
import functools

import jax
import jax.numpy as jnp
from jax import lax
from jax.experimental import pallas as pl
from jax.experimental.pallas import tpu as pltpu
from jax.sharding import PartitionSpec as P

SMOOTH = 17
water_level = 0.05
bf16 = jnp.bfloat16
f32 = jnp.float32
LANES = 128
LAG = 4


def split(x):
    hi = x.astype(bf16)
    return hi, (x - hi.astype(f32)).astype(bf16)


def build_toeplitz(bank_ref, toep):
    _, nbank, ntap = bank_ref.shape
    chans = toep.shape[1] // (2 * nbank)
    for b in range(nbank):
        parts = []
        for p in range(2):
            row = jnp.concatenate(
                [bank_ref[p, b : b + 1, :], jnp.zeros((1, LANES - ntap), f32)], axis=1
            )
            full = jnp.broadcast_to(row, (chans, LANES))
            parts.append(split(pltpu.roll(full, 0, 1, stride=1, stride_axis=0)))
        at = b * 2 * chans
        for part in range(2):
            real, imag = parts[0][part], parts[1][part]
            toep[part, at : at + chans, :LANES] = real
            toep[part, at : at + chans, LANES:] = -imag
            toep[part, at + chans : at + 2 * chans, :LANES] = imag
            toep[part, at + chans : at + 2 * chans, LANES:] = real


def build_window(band):
    bins = band.shape[0]
    rows = lax.broadcasted_iota(jnp.int32, (bins, bins), 0)
    cols = lax.broadcasted_iota(jnp.int32, (bins, bins), 1)
    band[...] = (jnp.abs(rows - cols) <= SMOOTH // 2).astype(f32).astype(bf16)


def filter_window(nbank, w, x, toep, index_ref, filt, power):
    bins = filt.shape[2]
    chans = toep.shape[1] // (2 * nbank)
    tile = 256
    rows = slice(w * chans, (w + 1) * chans)
    for n in range(bins // tile):
        cut = slice(n * tile, (n + 1) * tile)
        here = x(cut)
        res = jnp.dot(toep[0], here, preferred_element_type=f32)
        res += jnp.dot(toep[1], here, preferred_element_type=f32)
        index = index_ref[:, cut]
        acc = res[: 2 * chans]
        for b in range(1, nbank):
            acc = jnp.where(index == b, res[2 * chans * b : 2 * chans * (b + 1)], acc)
        real, imag = acc[:chans], acc[chans:]
        filt[0, rows, cut] = real
        filt[1, rows, cut] = imag
        hi, lo = split(real * real + imag * imag)
        power[0, rows, cut] = hi
        power[1, rows, cut] = lo


def whiten_window(w, band, mask_ref, filt, power):
    chans = mask_ref.shape[1]
    rows = slice(w * chans, (w + 1) * chans)
    smooth = jnp.dot(power[0, rows], band[...], preferred_element_type=f32)
    smooth += jnp.dot(power[1, rows], band[...], preferred_element_type=f32)
    scale = lax.rsqrt(smooth * (1.0 / SMOOTH) + water_level)
    eye = lax.broadcasted_iota(jnp.int32, (chans, chans), 0) == lax.broadcasted_iota(
        jnp.int32, (chans, chans), 1
    )
    row = jnp.broadcast_to(mask_ref[w : w + 1, :].astype(f32), (chans, chans))
    valid = jnp.sum(jnp.where(eye, row, 0.0), axis=1, keepdims=True)
    scale = scale * valid
    return [(filt[p, rows] * scale).astype(bf16) for p in range(2)]


class Line:
    def __init__(self, pos, length, device_of, lag, refs):
        self.pos, self.length, self.device_of, self.lag = pos, length, device_of, lag
        self.own, self.out_r, self.out_l, self.in_r, self.in_l, self.sems = refs
        self.count = self.own.shape[0]

    def clear(self):
        @pl.when(self.pos == 0)
        def _():
            self.in_r[...] = jnp.zeros_like(self.in_r)

        @pl.when(self.pos == self.length - 1)
        def _():
            self.in_l[...] = jnp.zeros_like(self.in_l)

    def copy(self, way, k):
        out, into = (self.out_r, self.in_r) if way == 0 else (self.out_l, self.in_l)
        other = self.pos + 1 if way == 0 else self.pos - 1
        return pltpu.make_async_remote_copy(
            src_ref=out.at[k],
            dst_ref=into.at[k],
            send_sem=self.sems.at[way, 0, k],
            recv_sem=self.sems.at[way, 1, k],
            device_id={"chan": self.device_of(other)},
            device_id_type=pl.DeviceIdType.MESH,
        )

    def tick(self, t):
        for way in range(2):
            behind = self.pos if way == 0 else self.length - 1 - self.pos
            out, into = (self.out_r, self.in_r) if way == 0 else (self.out_l, self.in_l)
            k = t - self.lag * behind
            inside = jnp.logical_and(k >= 0, k < self.count)

            @pl.when(jnp.logical_and(inside, behind > 0))
            def _(way=way, k=k):
                self.copy(way, k).wait_recv()

            @pl.when(jnp.logical_and(inside, behind < self.length - 1))
            def _(way=way, k=k, out=out, into=into):
                out[k] = self.own[k] + into[k]
                self.copy(way, k).start()

    def result(self, k):
        return self.own[k] + self.in_r[k] + self.in_l[k]

    def drain(self):
        for way in range(2):
            behind = self.pos if way == 0 else self.length - 1 - self.pos

            @pl.when(behind < self.length - 1)
            def _(way=way):
                @pl.loop(0, self.count)
                def _(k):
                    self.copy(way, k).wait_send()


def front_kernel(
    rows,
    cols,
    owner_ref,
    own_ref,
    bank_ref,
    index_ref,
    mask_ref,
    out_ref,
    src_ref,
    halo,
    toep,
    band,
    filt,
    power,
    mine,
    beside,
    row_buf,
    done,
    gathered,
    halo_sems,
    beside_sems,
    row_sems,
    gather_sems,
):
    wins, chans = mask_ref.shape
    bins = own_ref.shape[3]
    parts = 2 * cols
    subs, piece = beside.shape[1], beside.shape[2]
    me = lax.axis_index("chan")
    size = rows * cols * 2
    core = me % 2
    place = me % (2 * cols)
    base = me - place
    row = me // (2 * cols)
    partner = me + 1 - 2 * core
    mesh_id = pl.DeviceIdType.MESH

    barrier = pltpu.get_barrier_semaphore()
    partners = [
        (me > 0, me - 1),
        (me < size - 1, me + 1),
        (row > 0, me - 2 * cols),
        (row < rows - 1, me + 2 * cols),
    ] + [(place != j, base + j) for j in range(2 * cols)]
    expected = jnp.int32(0)
    for there, who in partners:
        expected += there.astype(jnp.int32)

        @pl.when(there)
        def _(who=who):
            pl.semaphore_signal(barrier, inc=1, device_id={"chan": who}, device_id_type=mesh_id)

    pl.semaphore_wait(barrier, expected)

    def halo_copy(way, w):
        return pltpu.make_async_remote_copy(
            src_ref=own_ref.at[:, w],
            dst_ref=halo.at[way, :, w],
            send_sem=halo_sems.at[way, 0, w],
            recv_sem=halo_sems.at[way, 1, w],
            device_id={"chan": me + 1 - 2 * way},
            device_id_type=mesh_id,
        )

    order = list(range(wins))
    sends = (me < size - 1, me > 0)
    for w in order:
        for way in range(2):

            @pl.when(sends[way])
            def _(way=way, w=w):
                halo_copy(way, w).start()

    for way in range(2):

        @pl.when(jnp.logical_not(sends[1 - way]))
        def _(way=way):
            halo[way] = jnp.zeros_like(halo[way])

    line = Line(row, rows, lambda i: i * 2 * cols + place, LAG, (*row_buf, row_sems))
    line.clear()
    build_toeplitz(bank_ref, toep)
    build_window(band)

    def beside_copy(sender, j):
        return pltpu.make_async_remote_copy(
            src_ref=mine.at[pl.ds(j * subs, subs)],
            dst_ref=beside.at[sender],
            send_sem=beside_sems.at[0, j],
            recv_sem=beside_sems.at[1, sender],
            device_id={"chan": base + j},
            device_id_type=mesh_id,
        )

    blank = jnp.zeros((LANES - 3 * chans, bins), bf16)
    for w in order:
        for way in range(2):

            @pl.when(sends[1 - way])
            def _(way=way, w=w):
                halo_copy(way, w).wait_recv()

        def x(cut, w=w):
            stack = []
            for p in range(2):
                stack += [halo[0, p, w, :, cut], own_ref[p, w, :, cut], halo[1, p, w, :, cut]]
                stack += [blank[:, cut]]
            return jnp.concatenate(stack, axis=0)

        filter_window(bank_ref.shape[1], w, x, toep, index_ref, filt, power)
        white = whiten_window(w, band, mask_ref, filt, power)
        for p in range(2):
            out_ref[p, w] = white[p]
            for i in range(chans // piece):
                mine[(w * 2 + p) * (chans // piece) + i] = white[p][i * piece : (i + 1) * piece]
        for j in range(w * parts // wins, (w + 1) * parts // wins):

            @pl.when(place != j)
            def _(j=j):
                beside_copy(place, j).start()

    beside[place] = mine[pl.ds(place * subs, subs)]
    for j in range(parts):

        @pl.when(place != j)
        def _(j=j):
            beside_copy(j, j).wait_recv()

    count = line.count

    @pl.loop(0, count)
    def _(k):
        total = jnp.zeros((piece, bins), bf16)
        for j in range(parts):
            total += beside[j, k % subs] * (owner_ref[k // subs] == base + j).astype(f32).astype(bf16)
        line.own[k] = total

    def give(src, origin, k, sem, who):
        return pltpu.make_async_remote_copy(
            src_ref=src,
            dst_ref=gathered.at[origin, k],
            send_sem=gather_sems.at[sem, k],
            recv_sem=gather_sems.at[2 * parts + origin, k],
            device_id={"chan": who},
            device_id_type=mesh_id,
        )

    def put(j, k, value):
        src_ref[k // subs, j * subs + k % subs] = value

    alike = [jnp.logical_and(place != j, core == j % 2) for j in range(parts)]
    last = LAG * (rows - 1)

    @pl.loop(0, count + last + LAG)
    def _(t):
        line.tick(t)
        k = t - last

        @pl.when(jnp.logical_and(k >= 0, k < count))
        def _():
            total = line.result(k)
            done[k] = total
            for j in range(parts):

                @pl.when(alike[j])
                def _(j=j):
                    give(done.at[k], place, k, j, base + j).start()

            give(done.at[k], place, k, parts + place, partner).start()
            put(place, k, total)

        q = t - last - LAG

        @pl.when(q >= 0)
        def _():
            for j in range(parts):

                @pl.when(alike[j])
                def _(j=j):
                    give(done.at[q], j, q, j, partner).wait_recv()
                    give(gathered.at[j, q], j, q, parts + j, partner).start()
                    put(j, q, gathered[j, q])

    @pl.loop(0, count)
    def _(k):
        for j in range(parts):

            @pl.when(core != j % 2)
            def _(j=j):
                give(done.at[k], j, k, j, partner).wait_recv()
                put(j, k, gathered[j, k])

    for way in range(2):
        for w in range(wins):

            @pl.when(sends[way])
            def _(way=way, w=w):
                halo_copy(way, w).wait_send()

    for j in range(parts):

        @pl.when(place != j)
        def _(j=j):
            beside_copy(place, j).wait_send()

    line.drain()

    @pl.loop(0, count)
    def _(k):
        give(done.at[k], place, k, parts + place, partner).wait_send()
        for j in range(parts):

            @pl.when(alike[j])
            def _(j=j):
                give(done.at[k], place, k, j, partner).wait_send()
                give(gathered.at[j, k], j, k, parts + j, partner).wait_send()


def front(grid, owner, own, bank, index, mask):
    _, wins, chans, bins = own.shape
    nbank = bank.shape[1]
    rounds = owner.shape[0]
    rows, cols = grid
    parts = 2 * cols
    total = wins * 2 * chans
    piece = min(chans, total // parts)
    subs = total // parts // piece
    count = rounds * subs
    vmem = pl.BlockSpec(memory_space=pltpu.VMEM)
    chunk = (piece, bins)
    chunks = pltpu.VMEM((count, *chunk), bf16)
    return pl.pallas_call(
        functools.partial(front_kernel, rows, cols),
        out_shape=[
            jax.ShapeDtypeStruct(own.shape, bf16),
            jax.ShapeDtypeStruct((rounds, parts * subs, piece, bins), bf16),
        ],
        in_specs=[pl.BlockSpec(memory_space=pltpu.SMEM)] + [vmem] * 4,
        out_specs=[vmem] * 2,
        scratch_shapes=[
            pltpu.VMEM((2, *own.shape), bf16),
            pltpu.VMEM((2, nbank * 2 * chans, 2 * LANES), bf16),
            pltpu.VMEM((bins, bins), bf16),
            pltpu.VMEM((2, wins * chans, bins), f32),
            pltpu.VMEM((2, wins * chans, bins), bf16),
            pltpu.VMEM((parts * subs, *chunk), bf16),
            pltpu.VMEM((parts, subs, *chunk), bf16),
            [chunks] * 5,
            chunks,
            pltpu.VMEM((parts, count, *chunk), bf16),
            pltpu.SemaphoreType.DMA((2, 2, wins)),
            pltpu.SemaphoreType.DMA((2, parts)),
            pltpu.SemaphoreType.DMA((2, 2, count)),
            pltpu.SemaphoreType.DMA((3 * parts, count)),
        ],
        compiler_params=pltpu.CompilerParams(collective_id=0, has_side_effects=True),
        name="front",
    )(owner, own, bank, index, mask)


def tree_sum(terms):
    while len(terms) > 1:
        terms = [a + b for a, b in zip(terms[::2], terms[1::2])]
    return terms[0]


def cross_kernel(offset_ref, src_ref, loc_ref, out_ref, wide, held):
    _, wins, chans, bins = loc_ref.shape
    count = out_ref.shape[1]
    r, h = pl.program_id(0), pl.program_id(1)

    @pl.when(jnp.logical_and(r == 0, h == 0))
    def _():
        held[...] = loc_ref[...]

    @pl.when(h == 0)
    def _():
        for p in range(2):
            for w in range(wins):
                wide[:, p * wins + w, :] = src_ref[0, w, p].astype(f32) * (1.0 / wins)

    for n in range(bins // LANES):
        cut = slice(n * LANES, (n + 1) * LANES)

        def one(j, carry, cut=cut):
            loc = [[held[p, w, :, cut] for w in range(wins)] for p in range(2)]
            at = offset_ref[r, h * count + j]
            src = [
                [
                    jnp.broadcast_to(
                        wide[at, p * wins + w : p * wins + w + 1, cut], (chans, LANES)
                    ).astype(bf16)
                    for w in range(wins)
                ]
                for p in range(2)
            ]
            real = tree_sum(
                [src[p][w] * loc[p][w] for w in range(wins) for p in range(2)]
            )
            plus = tree_sum([src[0][w] * loc[1][w] for w in range(wins)])
            minus = tree_sum([src[1][w] * loc[0][w] for w in range(wins)])
            out_ref[0, j, :, cut] = real
            out_ref[1, j, :, cut] = plus - minus
            return carry

        lax.fori_loop(0, count, one, 0, unroll=4)


def cross(offset, src, loc, blocks=1):
    rounds, wins, _, chans, bins = src.shape
    per = chans // blocks
    return pl.pallas_call(
        cross_kernel,
        out_shape=jax.ShapeDtypeStruct((2, rounds * chans, chans, bins), bf16),
        grid=(rounds, blocks),
        in_specs=[
            pl.BlockSpec(memory_space=pltpu.SMEM),
            pl.BlockSpec((1, wins, 2, chans, bins), lambda r, h: (r, 0, 0, 0, 0)),
            pl.BlockSpec((2, wins, chans, bins), lambda r, h: (0, 0, 0, 0)),
        ],
        out_specs=pl.BlockSpec((2, per, chans, bins), lambda r, h: (0, r * blocks + h, 0, 0)),
        scratch_shapes=[
            pltpu.VMEM((chans, 2 * wins, bins), f32),
            pltpu.VMEM((2, wins, chans, bins), bf16),
        ],
        name="cross",
    )(offset, src, loc)


def chip_grid(size):
    chips = size // 2
    cols = 1
    while cols * cols * 4 <= chips:
        cols *= 2
    return chips // cols, cols


UP, DOWN, SIDE, NEAR, LATE = 8, 8, 8, 4, 7


class Chain(Line):
    def copy(self, way, k):
        out, into = (self.out_r, self.in_r) if way == 0 else (self.out_l, self.in_l)
        other = self.pos + 1 if way == 0 else self.pos - 1
        return self.make(way, out.at[k], into.at[k], k, self.device_of(other))

    def make(self, way, src, dst, k, who):
        return pltpu.make_async_remote_copy(
            src_ref=src,
            dst_ref=dst,
            send_sem=self.sems.at[way, self.count],
            recv_sem=self.sems.at[way, k],
            device_id={"chan": who},
            device_id_type=pl.DeviceIdType.MESH,
        )

    def tick(self, t):
        for way in (1, 0):
            behind = self.pos if way == 0 else self.length - 1 - self.pos
            out, into = (self.out_r, self.in_r) if way == 0 else (self.out_l, self.in_l)
            k = t - self.lag[way] * behind
            inside = jnp.logical_and(k >= 0, k < self.count)

            @pl.when(jnp.logical_and(inside, behind > 0))
            def _(way=way, k=k):
                self.copy(way, k).wait_recv()

            @pl.when(jnp.logical_and(inside, behind < self.length - 1))
            def _(way=way, k=k, out=out, into=into):
                out[k] = self.own[k] + into[k]
                self.copy(way, k).start()

    def drain(self, who):
        for way in range(2):
            behind = self.pos if way == 0 else self.length - 1 - self.pos
            out = self.out_r if way == 0 else self.out_l

            @pl.when(behind < self.length - 1)
            def _(way=way, out=out):
                self.make(way, out, out, 0, who).wait_send()


def build_bank(bank_ref, toep):
    _, nbank, ntap = bank_ref.shape
    outs = toep.shape[0] // (2 * nbank)
    for b in range(nbank):
        parts = []
        for p in range(2):
            row = jnp.concatenate(
                [bank_ref[p, b : b + 1, :], jnp.zeros((1, LANES - ntap), f32)], axis=1
            )
            full = jnp.broadcast_to(row, (outs, LANES))
            parts.append(split(pltpu.roll(full, 0, 1, stride=1, stride_axis=0)))
        at = b * 2 * outs
        for part in range(2):
            real, imag = parts[0][part], parts[1][part]
            left = slice(2 * part * LANES, (2 * part + 1) * LANES)
            right = slice((2 * part + 1) * LANES, (2 * part + 2) * LANES)
            toep[at : at + outs, left] = real
            toep[at : at + outs, right] = -imag
            toep[at + outs : at + 2 * outs, left] = imag
            toep[at + outs : at + 2 * outs, right] = real


def build_band(band):
    wide, bins = band.shape
    rows = lax.broadcasted_iota(jnp.int32, (wide, bins), 0)
    cols = lax.broadcasted_iota(jnp.int32, (wide, bins), 1)
    band[...] = (jnp.abs(rows - bins - cols) <= SMOOTH // 2).astype(f32).astype(bf16)


def build_pick(base, place, owner_ref, offset_ref, masks, pick):
    parts, _, chans = masks.shape
    rounds = offset_ref.shape[0]
    total = parts * chans
    valid = jnp.concatenate(
        [masks[b, pl.ds(place, 1), :].astype(f32) for b in range(parts)], axis=1
    )
    eye = lax.broadcasted_iota(jnp.int32, (chans, chans), 0) == lax.broadcasted_iota(
        jnp.int32, (chans, chans), 1
    )
    cols = lax.broadcasted_iota(jnp.int32, (chans, total), 1).astype(f32)
    for r in range(rounds):
        row = jnp.broadcast_to(offset_ref[r : r + 1, :].astype(f32), (chans, chans))
        col = jnp.sum(jnp.where(eye, row, 0.0), axis=1, keepdims=True)
        col = col + ((owner_ref[r] - base) * chans).astype(f32)
        pick[r * chans : (r + 1) * chans] = jnp.where(cols == col, valid * (1.0 / parts), 0.0).astype(bf16)
    rows = lax.broadcasted_iota(jnp.int32, (total, total), 0)
    same = rows == lax.broadcasted_iota(jnp.int32, (total, total), 1)
    pick[rounds * chans :] = jnp.where(same, valid, 0.0).astype(bf16)


def filter_cuts(first, cuts, nbank, raw, toep, index_ref, filt, power):
    outs = toep.shape[0] // (2 * nbank)
    blocks, chans = raw.shape[1], raw.shape[3]
    step = outs // chans
    many = range(first, first + cuts)
    index = index_ref[:, first * LANES : (first + cuts) * LANES]
    for u in range((blocks - 2) // step):
        here = [
            raw[first // cuts, u * step : u * step + step + 2, p].reshape(
                (step + 2) * chans, cuts * LANES
            )
            for p in range(2)
        ]
        res = jnp.dot(
            toep[...], jnp.concatenate(here + here, axis=0), preferred_element_type=f32
        )
        acc = res[: 2 * outs]
        for b in range(1, nbank):
            acc = jnp.where(index == b, res[2 * outs * b : 2 * outs * (b + 1)], acc)
        real, imag = acc[:outs], acc[outs:]
        rows = slice(u * outs, (u + 1) * outs)
        for q in many:
            cut = slice((q - first) * LANES, (q - first + 1) * LANES)
            filt[q, 0, rows] = real[:, cut]
            filt[q, 1, rows] = imag[:, cut]
        power[rows, (first + 1) * LANES : (first + cuts + 1) * LANES] = (
            real * real + imag * imag
        ).astype(bf16)


def whiten_cut(q, band, pick, filt, power, own, mine):
    rounds = own.shape[0] // filt.shape[0]
    chans = own.shape[2]
    smooth = jnp.dot(
        power[:, q * LANES : (q + 3) * LANES], band[...], preferred_element_type=f32
    )
    scale = lax.rsqrt(smooth * (1.0 / SMOOTH) + water_level)
    white = jnp.concatenate([(filt[q, p] * scale).astype(bf16) for p in range(2)], axis=1)
    res = jnp.dot(pick[...], white, preferred_element_type=f32).astype(bf16)
    at = rounds * chans
    for p in range(2):
        cut = slice(p * LANES, (p + 1) * LANES)
        for r in range(rounds):
            own[q * rounds + r, p] = res[r * chans : (r + 1) * chans, cut]
        for b in range(mine.shape[1]):
            mine[q, b, p] = res[at + b * chans : at + (b + 1) * chans, cut]


def row_kernel(
    rows,
    owner_in,
    own_in,
    bank_in,
    index_in,
    mask_in,
    offset_in,
    loc_ref,
    src_ref,
    part_ref,
    owner_ref,
    own_ref,
    bank_ref,
    index_ref,
    mask_ref,
    offset_ref,
    in_sems,
    raw,
    masks,
    toep,
    band,
    pick,
    filt,
    power,
    mine,
    back,
    line_buf,
    done,
    across,
    beside,
    raw_send,
    raw_recv,
    mask_sems,
    back_sems,
    line_sems,
    give_sems,
    give_recv,
):
    wins, chans = mask_ref.shape
    halves, span = raw.shape[0], raw.shape[4]
    cuts = halves * span // LANES
    nbank = bank_ref.shape[1]
    parts = wins
    rounds = owner_ref.shape[0]
    me = lax.axis_index("chan")
    core = me % 2
    place = me % parts
    base = me - place
    row = me // parts
    partner = me + 1 - 2 * core
    alike = base + (place + 2) % parts
    partner_place = place + 1 - 2 * core
    alike_place = (place + 2) % parts
    corner_place = (partner_place + 2) % parts
    mesh_id = pl.DeviceIdType.MESH

    def send(src, dst, send_sem, recv_sem, who):
        return pltpu.make_async_remote_copy(
            src_ref=src,
            dst_ref=dst,
            send_sem=send_sem,
            recv_sem=recv_sem,
            device_id={"chan": who},
            device_id_type=mesh_id,
        )

    pairs_in = [
        (own_in, own_ref),
        (mask_in, mask_ref),
        (bank_in, bank_ref),
        (index_in, index_ref),
        (offset_in, offset_ref),
        (owner_in, owner_ref),
    ]
    inputs = [
        pltpu.make_async_copy(src, dst, in_sems.at[n]) for n, (src, dst) in enumerate(pairs_in)
    ]
    for copy in inputs:
        copy.start()

    barrier = pltpu.get_barrier_semaphore()
    partners = [(place != j, base + j) for j in range(parts)]
    for j in range(parts):
        near = jnp.logical_or(place == j, jnp.logical_or(place == parts - 1, j == 0))
        partners.append((jnp.logical_and(row < rows - 1, near), base + parts + j))
        near = jnp.logical_or(place == j, jnp.logical_or(place == 0, j == parts - 1))
        partners.append((jnp.logical_and(row > 0, near), base - parts + j))
    expected = jnp.int32(0)
    for there, who in partners:
        expected += there.astype(jnp.int32)

        @pl.when(there)
        def _(who=who):
            pl.semaphore_signal(barrier, inc=1, device_id={"chan": who}, device_id_type=mesh_id)

    pl.semaphore_wait(barrier, expected)

    peers = [alike_place, corner_place, partner_place]

    def raw_copy(q, to, slot, n, who):
        return send(
            own_ref.at[:, to, :, q * span : (q + 1) * span],
            raw.at[q, slot],
            raw_send.at[min(n // (parts - 1), 1)],
            raw_recv.at[q],
            who,
        )

    def mask_copy(n):
        return send(
            mask_ref, masks.at[place], mask_sems.at[0], mask_sems.at[1], base + peers[n]
        )

    above = jnp.logical_and(place == parts - 1, row < rows - 1)
    below = jnp.logical_and(place == 0, row > 0)

    def edges(q, act):
        @pl.when(above)
        def _():
            for j in range(parts):
                act(raw_copy(q, j, 0, parts - 1 + j, base + parts + j))

        @pl.when(below)
        def _():
            for j in range(parts):
                act(raw_copy(q, j, parts + 1, parts - 1 + j, base - parts + j))

    for copy in inputs:
        copy.wait()
    for n in range(parts - 1):
        mask_copy(n).start()
    for q in range(halves):
        for n in range(2):
            raw_copy(q, peers[n], 1 + place, n, base + peers[n]).start()
        edges(q, lambda copy: copy.start())
        raw_copy(q, peers[2], 1 + place, 2, base + peers[2]).start()

    masks[place] = mask_ref[...]
    for q in range(halves):
        raw[q, 1 + place] = own_ref[:, place, :, q * span : (q + 1) * span]

    @pl.when(row == 0)
    def _():
        raw[:, 0] = jnp.zeros_like(raw[:, 0])

    @pl.when(row == rows - 1)
    def _():
        raw[:, parts + 1] = jnp.zeros_like(raw[:, parts + 1])

    line = Chain(row, rows, lambda i: i * parts + place, (UP, DOWN), (*line_buf, line_sems))
    line.clear()
    build_bank(bank_ref, toep)
    build_band(band)
    edge = jnp.zeros((power.shape[0], LANES), bf16)
    power[:, :LANES] = edge
    power[:, (cuts + 1) * LANES :] = edge

    def whole(ref, send_sem, recv_sem):
        return send(ref, ref, send_sem, recv_sem, partner)

    whole(masks.at[: parts - 1], mask_sems.at[0], mask_sems.at[1]).wait_recv()
    build_pick(base, place, owner_ref, offset_ref, masks, pick)

    some = back.at[:, : parts - 1]
    count = line.count
    last = jnp.maximum(jnp.maximum(UP * row, DOWN * (rows - 1 - row)), count)
    longest = max(max(UP, DOWN) * (rows - 1), count)

    def give(src, dst, n, k, who):
        return send(src.at[k], dst, give_sems.at[n], give_recv.at[(n + 1) // 2, k], who)

    def put(k, j, value):
        src_ref[k, j] = value.astype(f32)

    def tick(t):
        line.tick(t)
        k = t - last

        @pl.when(jnp.logical_and(k >= 0, k < count))
        def _():
            total = line.result(k)
            done[k] = total
            give(done, across.at[k], 0, k, alike).start()
            give(done, beside.at[k, 0], 1, k, partner).start()
            put(k, place, total)

        q = t - last - SIDE

        @pl.when(jnp.logical_and(q >= 0, q < count))
        def _():
            give(done, across.at[q], 0, q, alike).wait_recv()
            give(across, beside.at[q, 1], 2, q, partner).start()
            put(q, alike_place, across[q])

        b = t - last - SIDE - NEAR

        @pl.when(jnp.logical_and(b >= 0, b < count))
        def _():
            whole(beside.at[b], give_sems.at[1], give_recv.at[1, b]).wait_recv()
            put(b, partner_place, beside[b, 0])
            put(b, corner_place, beside[b, 1])

        @pl.when(b == 0)
        def _():
            whole(some, back_sems.at[0], back_sems.at[1]).wait_recv()
            loc_ref[...] = back[...]

        @pl.when(jnp.logical_and(b >= 0, b < count - LATE))
        def _():
            at, r = b // rounds, b % rounds
            cut = pl.ds(pl.multiple_of(at * LANES, LANES), LANES)
            loc = [[back[at, w, p] for w in range(wins)] for p in range(2)]

            def wide(w, p, j):
                return src_ref[b, w, p, pl.ds(j, 1), :]

            def keep(j, real, imag):
                part_ref[0, r * chans + j, :, cut] = real
                part_ref[1, r * chans + j, :, cut] = imag

            products(wide, loc, keep, chans)

    def back_copy(q, n):
        return send(
            mine.at[q, peers[n]],
            back.at[q, place],
            back_sems.at[0],
            back_sems.at[1],
            base + peers[n],
        )

    def pass_on(q):
        back[q, place] = mine[q, place]

        @pl.loop(q * rounds, (q + 1) * rounds)
        def _(t):
            line.tick(t)

        for n in range(parts - 1):
            back_copy(q, n).start()

    def finish(q):
        whiten_cut(q, band, pick, filt, power, line.own, mine)
        pass_on(q)

    inner = jnp.logical_and(row > 0, row < rows - 1)
    outer = jnp.logical_or(row == 0, row == rows - 1)
    half = cuts // halves
    for first in range(0, cuts, half):
        for there, many in ((inner, parts + 1), (outer, parts)):

            @pl.when(there)
            def _(q=first // half, many=many):
                whole(raw.at[q, :many], raw_send.at[0], raw_recv.at[q]).wait_recv()

        filter_cuts(first, half, nbank, raw, toep, index_ref, filt, power)
        if first == 0:
            for q in range(half - 1):
                finish(q)
    for q in range(half - 1, cuts):
        whiten_cut(q, band, pick, filt, power, line.own, mine)
    for q in range(half - 1, cuts):
        pass_on(q)

    @pl.loop(cuts * rounds, count + longest + SIDE + NEAR)
    def _(t):
        tick(t)

    whole(some, back_sems.at[0], back_sems.at[1]).wait_send()
    whole(masks.at[: parts - 1], mask_sems.at[0], mask_sems.at[1]).wait_send()
    whole(raw.at[:, : parts - 1], raw_send.at[0], raw_recv.at[0]).wait_send()

    @pl.when(jnp.logical_or(above, below))
    def _():
        whole(raw.at[:, :parts], raw_send.at[1], raw_recv.at[0]).wait_send()

    line.drain(partner)
    for n in range(3):
        whole(done, give_sems.at[n], give_recv.at[0, 0]).wait_send()


def row_front(rows, owner, own, bank, index, mask, offset):
    _, wins, chans, bins = own.shape
    nbank = bank.shape[1]
    rounds = owner.shape[0]
    cuts = bins // LANES
    parts = wins
    count = cuts * rounds
    outs = LANES // 2
    vmem = pl.BlockSpec(memory_space=pltpu.VMEM)
    chunk = (2, chans, LANES)
    chunks = pltpu.VMEM((count, *chunk), bf16)
    return pl.pallas_call(
        functools.partial(row_kernel, rows),
        out_shape=[
            pltpu.VMEM((cuts, wins, *chunk), bf16),
            pltpu.VMEM((count, wins, *chunk), f32),
            pltpu.VMEM((2, rounds * chans, chans, bins), bf16),
        ],
        in_specs=[pl.BlockSpec(memory_space=pltpu.HBM)] * 6,
        out_specs=[vmem] * 3,
        scratch_shapes=[
            pltpu.SMEM(owner.shape, owner.dtype),
            *[pltpu.VMEM(a.shape, a.dtype) for a in (own, bank, index, mask, offset)],
            pltpu.SemaphoreType.DMA((6,)),
            pltpu.VMEM((2, parts + 2, 2, chans, bins // 2), bf16),
            pltpu.VMEM((parts, wins, chans), jnp.int32),
            pltpu.VMEM((nbank * 2 * outs, 4 * LANES), bf16),
            pltpu.VMEM((3 * LANES, LANES), bf16),
            pltpu.VMEM(((rounds + parts) * chans, parts * chans), bf16),
            pltpu.VMEM((cuts, 2, parts * chans, LANES), f32),
            pltpu.VMEM((parts * chans, (cuts + 2) * LANES), bf16),
            pltpu.VMEM((cuts, parts, *chunk), bf16),
            pltpu.VMEM((cuts, parts, *chunk), bf16),
            [chunks] * 5,
            chunks,
            chunks,
            pltpu.VMEM((count, 2, *chunk), bf16),
            pltpu.SemaphoreType.DMA((2,)),
            pltpu.SemaphoreType.DMA((2,)),
            pltpu.SemaphoreType.DMA((2,)),
            pltpu.SemaphoreType.DMA((2,)),
            pltpu.SemaphoreType.DMA((2, count + 1)),
            pltpu.SemaphoreType.DMA((3,)),
            pltpu.SemaphoreType.DMA((2, count)),
        ],
        compiler_params=pltpu.CompilerParams(
            collective_id=0, has_side_effects=True, vmem_limit_bytes=24 << 20
        ),
        name="front",
    )(*[pltpu.with_memory_space_constraint(a, pltpu.HBM) for a in (owner, own, bank, index, mask, offset)])


def products(wide, loc, put, count):
    wins = len(loc[0])
    chans = loc[0][0].shape[0]

    def one(j, carry):
        src = [
            [
                jnp.broadcast_to(wide(w, p, j), (chans, LANES)).astype(bf16)
                for w in range(wins)
            ]
            for p in range(2)
        ]
        real = tree_sum([src[p][w] * loc[p][w] for w in range(wins) for p in range(2)])
        plus = tree_sum([src[0][w] * loc[1][w] for w in range(wins)])
        minus = tree_sum([src[1][w] * loc[0][w] for w in range(wins)])
        put(j, real, plus - minus)
        return carry

    lax.fori_loop(0, count, one, 0, unroll=32)


def pairs_kernel(src_ref, loc_ref, part_ref, out_ref, buf, sems):
    cuts, wins, _, chans, _ = loc_ref.shape
    count = src_ref.shape[0]
    rounds = count // cuts
    first = count - buf.shape[0]

    def place_of(k, many=1):
        q, r = k // rounds, k % rounds
        rows = slice(r * chans, (r + many) * chans)
        return (slice(None), rows, slice(None), slice(q * LANES, (q + 1) * LANES))

    copies = []
    for k in range(0, first, rounds):
        at = place_of(k, min(rounds, first - k))
        copies.append(
            pltpu.make_async_copy(part_ref.at[at], out_ref.at[at], sems.at[len(copies)])
        )
        copies[-1].start()
    for k in range(first, count):
        loc = [[loc_ref[k // rounds, w, p] for w in range(wins)] for p in range(2)]

        def wide(w, p, j, k=k):
            return src_ref[k, w, p, pl.ds(j, 1), :]

        def put(j, real, imag, k=k):
            buf[k - first, 0, j] = real
            buf[k - first, 1, j] = imag

        products(wide, loc, put, chans)
        copies.append(
            pltpu.make_async_copy(
                buf.at[k - first], out_ref.at[place_of(k)], sems.at[len(copies)]
            )
        )
        copies[-1].start()
    for copy in copies:
        copy.wait()


def pairs(src, loc, part):
    cuts, _, _, chans, _ = loc.shape
    count = src.shape[0]
    late = min(LATE, count)
    vmem = pl.BlockSpec(memory_space=pltpu.VMEM)
    return pl.pallas_call(
        pairs_kernel,
        out_shape=jax.ShapeDtypeStruct(part.shape, bf16),
        in_specs=[vmem] * 3,
        out_specs=pl.BlockSpec(memory_space=pl.ANY),
        scratch_shapes=[
            pltpu.VMEM((late, 2, chans, chans, LANES), bf16),
            pltpu.SemaphoreType.DMA((cuts + late,)),
        ],
        compiler_params=pltpu.CompilerParams(vmem_limit_bytes=16 << 20),
        name="pairs",
    )(src, loc, part)


def body(spectra, filter_bank, band_index, window_mask, owner_order, source_offset):
    grid = chip_grid(lax.axis_size("chan"))
    _, wins, chans, bins = spectra.shape
    ntap = filter_bank.shape[2]
    if 2 * grid[1] == wins == 4 and 4 * chans == LANES and ntap == 2 * chans + 1:
        whitened, sources, part = row_front(
            grid[0],
            owner_order,
            spectra,
            filter_bank,
            band_index[None, :],
            window_mask,
            source_offset,
        )
        return pairs(sources, whitened, part)
    whitened, sources = front(
        grid, owner_order, spectra, filter_bank, band_index[None, :], window_mask
    )
    sources = sources.reshape(sources.shape[0], wins, 2, chans, bins)
    return cross(source_offset, sources, whitened)


def solution(mesh):
    in_specs = (
        P(None, "groups", "chan", None),
        P(),
        P(),
        P("groups", "chan"),
        P("groups"),
        P("groups", None),
    )
    out_specs = P(None, "groups", "chan", None)
    return jax.shard_map(body, mesh=mesh, in_specs=in_specs, out_specs=out_specs, check_vma=False)
```
